32 devices in a mesh: space: 8 (over z, core), ray: 4 (over y, x).
Axes of the slice: x: 2, y: 2, z: 4, core: 2. Of those that a mesh axis runs over, the one named last changes fastest.
Arguments:
- grid_table: bfloat16 [8, 4096, 256], P('space'), may hold values from -6 to 6
- weights: bfloat16 [8, 4, 256, 256], P('space'), may hold values from -0.375 to 0.375
- biases: float32 [8, 4, 256], P('space'), may hold values from -1.5 to 1.5
- density_head: float32 [8, 256], P('space'), may hold values from -0.375 to 0.375
- sample_cells: int32 [8, 2048, 8], P('space', 'ray'), may hold values from 0 to 4095
- sample_counts: int32 [2048, 8], P('ray', 'space'), may hold values from 0 to 8
- ray_order: int32 [2048, 8], P('ray'), may hold values from 0 to 7, each once within a row
- cotangent: float32 [2048, 256], P('ray'), may hold values from -6 to 6
Outputs:
- composite: float32 [2048, 256], P(('ray', 'space'))
- weight_grads: float32 [8, 4, 256, 256], P('space')
- bias_grads: float32 [8, 4, 256], P('space')
- head_grads: float32 [8, 256], P('space')
The draws below stay inside these ranges and needn't reach their ends.
Inputs may be any that keep to these rules, and one draw needn't show every extreme that they name: `ray_order`: each row is a permutation of 0 .. 7: the order in which the ray meets the partitions. `sample_counts`: A count of 0 means that the ray does not touch the partition.
All inputs are finite; a program needn't handle non-finite values.
Results may differ from the reference program's by a relative error of at most 0.0065.
The reference program's roundings to bfloat16 on the way count: a program that leaves them out, or rounds other values in their place, can miss the bound.
Values sent between devices are 32-bit elements; how exact they have to be, the bound alone decides.
No kernel may reach another device: no remote copies, remote signals or barrier semaphores. Data moves between devices by JAX's collectives and lax.ppermute only.
A program may use at most 128 MiB of HBM per device.

```python
import jax
import jax.numpy as jnp
from jax import lax

W = 256
LAYERS = 4
SAMPLES = 8
CELLS = 4096
PARTS_SIZE = 8
RAYS = 2048


def with_ends(drawn, stream_key, smallest, top_value):
    dims = drawn.shape
    place = [jax.random.randint(jax.random.fold_in(stream_key, axis), (), 0, dims[axis]) for axis in range(len(dims))]
    drawn = drawn.at[tuple(place)].set(smallest)
    longest = dims.index(max(dims))
    place[longest] = (place[longest] + 1) % dims[longest]
    return drawn.at[tuple(place)].set(top_value)


def steps_of(key, dims, pieces, low, top_value):
    def one(axis_at, blocks):
        heights = jax.random.uniform(jax.random.fold_in(jax.random.fold_in(key, 6), axis_at), (blocks,), jnp.float32, low / len(pieces), top_value / len(pieces))
        return jnp.repeat(jnp.exp(heights), dims[axis_at] // blocks).reshape((-1,) + (1,) * (len(dims) - axis_at - 1))

    loudness = one(*pieces[0])
    for cut in pieces[1:]:
        loudness = loudness * one(*cut)
    return loudness


def normal_values(own_key, extent, scale, reach, pieces=(), held_as=jnp.bfloat16):
    array = jax.random.normal(own_key, extent, jnp.float32) * scale
    if len(pieces) > 0:
        array = steps_of(own_key, extent, pieces, -0.22, 0.18) * array
    return jnp.clip(array, min=-reach, max=reach).astype(held_as)


def setup_inputs(seed: int = 0) -> dict:
    seeds = jax.random.split(jax.random.key(seed), 9)
    grid_table = normal_values(seeds[0], (PARTS_SIZE, CELLS, W), 1.0, 6.0, ((0, 8),))
    weights = normal_values(seeds[1], (PARTS_SIZE, LAYERS, W, W), W ** -0.5, 0.375, ((0, 8),))
    biases = normal_values(seeds[2], (PARTS_SIZE, LAYERS, W), 0.3, 1.5, ((0, 8),), jnp.float32)
    density_head = normal_values(seeds[3], (PARTS_SIZE, W), W ** -0.5, 0.375, ((0, 8),), jnp.float32)
    sample_cells = with_ends(jax.random.randint(seeds[4], (PARTS_SIZE, RAYS, SAMPLES), 0, CELLS), jax.random.fold_in(seeds[4], 1), 0, CELLS - 1).astype(jnp.int32)
    sample_counts = with_ends(jax.random.randint(seeds[5], (RAYS, PARTS_SIZE), 0, SAMPLES + 1), jax.random.fold_in(seeds[5], 1), 0, SAMPLES).astype(jnp.int32)
    ray_order = jax.vmap(lambda own: jax.random.permutation(own, PARTS_SIZE))(jax.random.split(seeds[6], RAYS)).reshape((RAYS, PARTS_SIZE)).astype(jnp.int32)
    cotangent = normal_values(seeds[7], (RAYS, W), 1.0, 6.0, ((0, 4),), jnp.float32)
    return {"grid_table": grid_table, "weights": weights, "biases": biases, "density_head": density_head, "sample_cells": sample_cells, "sample_counts": sample_counts, "ray_order": ray_order, "cotangent": cotangent}


step_length = 0.05

def forward(table, layer_mats, layer_bias, cells):
    hidden = table[cells.reshape(-1)]
    layer_inputs = []
    pre_acts = []
    linear = None
    for layer in range(layer_mats.shape[0]):
        layer_inputs.append(hidden)
        linear = jnp.dot(hidden, layer_mats[layer], preferred_element_type=jnp.float32) + layer_bias[layer]
        pre_acts.append(linear)
        if layer + 1 < layer_mats.shape[0]:
            hidden = jax.nn.relu(linear).astype(jnp.bfloat16)
    return (layer_inputs, pre_acts, linear)

def segment(features, head, count):
    slots = count.shape[0]
    width = features.shape[1]
    samples = features.shape[0] // slots
    logits = jnp.dot(features, head, precision=lax.Precision.HIGHEST)
    density = jax.nn.softplus(logits).reshape(slots, samples)
    live = lax.iota(jnp.int32, samples)[None, :] < count[:, None]
    optical = jnp.where(live, density * step_length, jnp.float32(0.0))
    before = jnp.cumsum(optical, axis=1) - optical
    blend = jnp.exp(-before) * (1.0 - jnp.exp(-optical))
    colour = jnp.einsum('rs,rsw->rw', blend, features.reshape(slots, samples, width), precision=lax.Precision.HIGHEST)
    decay = -lax.optimization_barrier(jnp.sum(optical, axis=1))
    return (colour, decay)

def backward(layer_inputs, pre_acts, layer_mats, grad_features):
    grad_linear = grad_features
    mats = []
    offsets = []
    for layer in range(layer_mats.shape[0] - 1, -1, -1):
        grad_half = grad_linear.astype(jnp.bfloat16)
        mats.append(lax.dot_general(layer_inputs[layer], grad_half, (((0,), (0,)), ((), ())), preferred_element_type=jnp.float32))
        offsets.append(lax.optimization_barrier(jnp.sum(grad_linear, axis=0)))
        if layer > 0:
            back = lax.dot_general(grad_half, layer_mats[layer], (((1,), (1,)), ((), ())), preferred_element_type=jnp.float32)
            grad_linear = back * (pre_acts[layer - 1] > 0).astype(jnp.float32)
    return (jnp.stack(mats[::-1]), jnp.stack(offsets[::-1]))

def reference(grid_table, weights, biases, density_head, sample_cells, sample_counts, ray_order, cotangent):
    parts = grid_table.shape[0]

    def first(index):
        layer_inputs, pre_acts, features = forward(grid_table[index], weights[index], biases[index], sample_cells[index])
        return segment(features, density_head[index], sample_counts[:, index])
    colours, decays = lax.map(first, jnp.arange(parts, dtype=jnp.int32))
    products = lax.optimization_barrier(jnp.sum(colours * cotangent[None, :, :], axis=2))
    ranks = ray_order.T
    earlier = ranks[None, :, :] < ranks[:, None, :]
    later = ranks[None, :, :] > ranks[:, None, :]
    prefix = jnp.exp(lax.optimization_barrier(jnp.sum(jnp.where(earlier, decays[None, :, :], jnp.float32(0.0)), axis=1)))
    shares = prefix * products
    tails = lax.optimization_barrier(jnp.sum(jnp.where(later, shares[None, :, :], jnp.float32(0.0)), axis=1))
    composite = lax.optimization_barrier(jnp.sum(prefix[:, :, None] * colours, axis=0))

    def second(index):
        layer_inputs, pre_acts, features = forward(grid_table[index], weights[index], biases[index], sample_cells[index])
        count = sample_counts[:, index]
        outputs, pull = jax.vjp(lambda feats, head: segment(feats, head, count), features, density_head[index])
        grad_features, grad_head = pull((prefix[index][:, None] * cotangent, tails[index]))
        mats, offsets = backward(layer_inputs, pre_acts, weights[index], grad_features)
        return (mats, offsets, grad_head)
    weight_grads, bias_grads, head_grads = lax.map(second, jnp.arange(parts, dtype=jnp.int32))
    return (composite, weight_grads, bias_grads, head_grads)
```

```python
import functools

import jax
import jax.numpy as jnp
from jax import lax
from jax.experimental import pallas as pl
from jax.experimental.pallas import tpu as pltpu
from jax.sharding import PartitionSpec as P

step_length = 0.05
RAY_BLOCK = 128
GATHER_UNROLL = 32

F32 = jnp.float32
BF16 = jnp.bfloat16
VMEM = pl.BlockSpec(memory_space=pltpu.VMEM)
SMEM = pl.BlockSpec(memory_space=pltpu.SMEM)


def columns(rows, block):
    n = rows.shape[0]
    square = jnp.concatenate([rows, jnp.zeros((block - n, block), F32)], axis=0).T
    return [square[:, i : i + 1] for i in range(n)]


def row_block(cols, block):
    lane = lax.broadcasted_iota(jnp.int32, (block, block), 1)
    square = jnp.zeros((block, block), F32)
    for i, col in enumerate(cols):
        square = jnp.where(lane == i, col, square)
    return square.T[: len(cols)]


def before_of(optical):
    slots = optical.shape[0]
    place = lax.broadcasted_iota(jnp.int32, optical.shape, 0)
    total = jnp.zeros_like(optical)
    for j in range(slots - 1):
        total = total + jnp.where(place > j, optical[j : j + 1], 0.0)
    return total


def forward_kernel(
    space_ref, cells_ref, counts_ref, order_ref, table_ref, mats_ref, bias_ref, head_ref, cot_ref,
    hidden_ref, feat_ref, logit_ref, side_ref, pack_ref, rel_ref, colour_ref,
    wide_table, rows_ref,
):
    layers, width = bias_ref.shape
    slots, rays = cells_ref.shape
    parts = order_ref.shape[0]
    block = RAY_BLOCK
    span = slots * block
    cells_per = 256

    @pl.loop(0, table_ref.shape[0] // cells_per)
    def _(t):
        at = pl.ds(pl.multiple_of(t * cells_per, cells_per), cells_per)
        wide_table[at, :] = table_ref[at, :].astype(F32)

    me = space_ref[0]
    for k in range(parts):
        rel_ref[k : k + 1, :] = order_ref[pl.ds(me ^ k, 1), :]

    head = head_ref[...]

    @pl.loop(0, rays // block)
    def _(c):
        first_ray = pl.multiple_of(c * block, block)

        @pl.loop(0, slots)
        def _(i):
            @pl.loop(0, block // GATHER_UNROLL)
            def _(j):
                base = j * GATHER_UNROLL
                for u in range(GATHER_UNROLL):
                    cell = cells_ref[i, first_ray + base + u]
                    rows_ref[pl.ds(i * block + base + u, 1), :] = wide_table[pl.ds(cell, 1), :]

        at = pl.ds(pl.multiple_of(c * span, span), span)
        ray_at = pl.ds(first_ray, block)
        hidden = rows_ref[...].astype(BF16)
        linear = None
        for layer in range(layers):
            hidden_ref[layer, at, :] = hidden
            linear = jnp.dot(hidden, mats_ref[layer], preferred_element_type=F32) + bias_ref[layer : layer + 1, :]
            if layer + 1 < layers:
                hidden = jnp.maximum(linear, 0.0).astype(BF16)
        feat_ref[at, :] = linear
        cot = cot_ref[ray_at, :]
        cols = []
        for i in range(slots):
            cols.append(jnp.sum(linear[i * block : (i + 1) * block] * head, axis=1, keepdims=True))
        for i in range(slots):
            cols.append(jnp.sum(linear[i * block : (i + 1) * block] * cot, axis=1, keepdims=True))
        both = row_block(cols, block)
        logit = both[:slots]
        side = both[slots:]
        density = jnp.maximum(logit, 0.0) + jnp.log1p(jnp.exp(-jnp.abs(logit)))
        place = lax.broadcasted_iota(jnp.int32, (slots, block), 0)
        live = place < counts_ref[:, ray_at]
        optical = jnp.where(live, density * step_length, 0.0)
        blend = jnp.exp(-before_of(optical)) * (1.0 - jnp.exp(-optical))
        logit_ref[:, ray_at] = logit
        side_ref[:, ray_at] = side
        decay = -jnp.sum(optical, axis=0, keepdims=True)
        product = jnp.sum(blend * side, axis=0, keepdims=True)
        pack_ref[0:1, ray_at] = decay
        pack_ref[1:2, ray_at] = product
        colour = jnp.zeros((block, width), F32)
        for i, col in enumerate(columns(blend, block)):
            colour = colour + col * linear[i * block : (i + 1) * block]
        colour_ref[ray_at, :] = colour


def layer_back(half, below, mats, layer):
    back = lax.dot_general(half, mats[layer], (((1,), (1,)), ((), ())), preferred_element_type=F32)
    return jnp.where(below > 0, back, 0.0)


def mat_grad(below, half):
    return lax.dot_general(below, half, (((0,), (0,)), ((), ())), preferred_element_type=F32)


def store_pieces(pieces_ref, slot, total, me):
    count = pieces_ref.shape[0]
    rows = total.shape[0] // count
    for owner in range(count):
        pieces_ref[pl.ds(owner ^ me, 1), slot * rows : (slot + 1) * rows, :] = total[owner * rows : (owner + 1) * rows][None]


def top_kernel(
    ray_ref, gathered_ref, rel_ref, counts_ref, logit_ref, side_ref, cot_ref, colour_ref, head_ref, mats_ref, hidden_ref, feat_ref,
    pieces_ref, half_ref, sums_ref, shaded_ref,
    acc_top, acc_next,
):
    layers = mats_ref.shape[0]
    top = layers - 1
    slots, rays = logit_ref.shape
    parts = rel_ref.shape[0]
    width = head_ref.shape[1]
    block = RAY_BLOCK
    span = slots * block
    head = head_ref[...]
    acc_top[...] = jnp.zeros_like(acc_top)
    acc_next[...] = jnp.zeros_like(acc_next)
    sums_ref[...] = jnp.zeros_like(sums_ref)

    @pl.loop(0, rays // block)
    def _(c):
        first_ray = pl.multiple_of(c * block, block)
        ray_at = pl.ds(first_ray, block)
        rank = rel_ref[:, ray_at]
        decays = gathered_ref[:, 0, ray_at]
        products = gathered_ref[:, 1, ray_at]
        ahead = jnp.zeros((parts, block), F32)
        for q in range(parts):
            ahead = ahead + jnp.where(rank[q : q + 1] < rank, decays[q : q + 1], 0.0)
        prefixes = jnp.exp(ahead)
        share = prefixes * products
        tail = jnp.sum(jnp.where(rank > rank[0:1], share, 0.0), axis=0, keepdims=True)
        prefix = prefixes[0:1]

        logit = logit_ref[:, ray_at]
        grown = jnp.exp(-jnp.abs(logit))
        density = jnp.maximum(logit, 0.0) + jnp.log1p(grown)
        slope = jnp.where(logit >= 0, 1.0, grown) / (1.0 + grown)
        place = lax.broadcasted_iota(jnp.int32, (slots, block), 0)
        live = place < counts_ref[:, ray_at]
        optical = jnp.where(live, density * step_length, 0.0)
        reach = jnp.exp(-before_of(optical))
        passed = jnp.exp(-optical)
        blend = reach * (1.0 - passed)
        grad_blend = prefix * side_ref[:, ray_at]
        lost = blend * grad_blend
        after = jnp.zeros_like(lost)
        for j in range(1, slots):
            after = after + jnp.where(place < j, lost[j : j + 1], 0.0)
        grad_optical = reach * passed * grad_blend - after - tail
        grad_logit = jnp.where(live, grad_optical * step_length, 0.0) * slope
        cols = columns(jnp.concatenate([blend * prefix, grad_logit, prefix, jnp.zeros((7, block), F32)], axis=0), block)
        cot = cot_ref[ray_at, :]
        shaded_ref[ray_at, :] = cols[2 * slots] * colour_ref[ray_at, :]
        at = pl.ds(pl.multiple_of(c * span, span), span)
        feats = feat_ref[at, :]
        grads = []
        head_sum = jnp.zeros((block, width), F32)
        bias_sum = jnp.zeros((block, width), F32)
        for i in range(slots):
            grad = cols[i] * cot + cols[slots + i] * head
            bias_sum = bias_sum + grad
            head_sum = head_sum + cols[slots + i] * feats[i * block : (i + 1) * block]
            grads.append(grad.astype(BF16))
        sums_ref[0:1, :] += jnp.sum(bias_sum, axis=0, keepdims=True)
        sums_ref[1:2, :] += jnp.sum(head_sum, axis=0, keepdims=True)
        half = jnp.concatenate(grads, axis=0)
        below = hidden_ref[top, at, :]
        acc_top[...] += mat_grad(below, half)
        grad = layer_back(half, below, mats_ref, top)
        sums_ref[2:3, :] += jnp.sum(grad, axis=0, keepdims=True)
        half = grad.astype(BF16)
        half_ref[at, :] = half
        acc_next[...] += mat_grad(hidden_ref[top - 1, at, :], half)

    me = ray_ref[0]
    store_pieces(pieces_ref, 0, acc_top[...], me)
    store_pieces(pieces_ref, 1, acc_next[...], me)


def low_kernel(ray_ref, half_ref, sums_ref, mats_ref, hidden_ref, pieces_ref, acc_a, acc_b, bias_ref):
    rows = half_ref.shape[0]
    span = 1024
    acc_a[...] = jnp.zeros_like(acc_a)
    acc_b[...] = jnp.zeros_like(acc_b)
    bias_ref[...] = jnp.zeros_like(bias_ref)

    @pl.loop(0, rows // span)
    def _(c):
        at = pl.ds(pl.multiple_of(c * span, span), span)
        grad = layer_back(half_ref[at, :], hidden_ref[2, at, :], mats_ref, 2)
        bias_ref[0:1, :] += jnp.sum(grad, axis=0, keepdims=True)
        half = grad.astype(BF16)
        below = hidden_ref[1, at, :]
        acc_a[...] += mat_grad(below, half)
        grad = layer_back(half, below, mats_ref, 1)
        bias_ref[1:2, :] += jnp.sum(grad, axis=0, keepdims=True)
        half = grad.astype(BF16)
        acc_b[...] += mat_grad(hidden_ref[0, at, :], half)

    me = ray_ref[0]
    store_pieces(pieces_ref, 0, acc_a[...], me)
    store_pieces(pieces_ref, 1, acc_b[...], me)
    count = pieces_ref.shape[0]
    first = 2 * (acc_a.shape[0] // count)
    small = jnp.concatenate(
        [sums_ref[0:3, :], bias_ref[0:2, :], jnp.zeros((3, acc_a.shape[1]), F32)], axis=0
    )
    for k in range(count):
        pieces_ref[k, first : first + 8, :] = small


def join_kernel(ray_ref, *refs):
    *pieces, out_ref = refs
    me = ray_ref[0]
    layers, width = out_ref.shape[:2]
    count = len(pieces) // 2
    rows = width // count
    for chunk in range(2):
        for k in range(count):
            piece = pieces[chunk * count + k]
            at = pl.ds(pl.multiple_of((me ^ k) * rows, rows), rows)
            for slot in range(2):
                out_ref[layers - 1 - 2 * chunk - slot, at, :] = piece[slot * rows : (slot + 1) * rows, :]


def partners(count, k):
    return [(i, i ^ k) for i in range(count)]


def on_device(
    grid_table, weights, biases, density_head, sample_cells, sample_counts, ray_order, cotangent
):
    table = grid_table[0]
    mats = weights[0]
    bias = biases[0]
    cells = sample_cells[0].T
    counts = sample_counts.T
    order = ray_order.T
    space = lax.axis_index("space")
    ray = lax.axis_index("ray")
    parts = lax.axis_size("space")
    ray_parts = lax.axis_size("ray")
    space_at = space.astype(jnp.int32)[None]
    ray_at = ray.astype(jnp.int32)[None]
    layers, width = bias.shape
    slots, rays = cells.shape
    rows = slots * rays
    shape = jax.ShapeDtypeStruct

    hidden, feats, logit, side, pack, rel, colour = pl.pallas_call(
        forward_kernel,
        out_shape=(
            shape((layers, rows, width), BF16),
            shape((rows, width), F32),
            shape((slots, rays), F32),
            shape((slots, rays), F32),
            shape((2, rays), F32),
            shape((parts, rays), jnp.int32),
            shape((rays, width), F32),
        ),
        in_specs=[SMEM, SMEM] + [VMEM] * 7,
        out_specs=(VMEM,) * 7,
        scratch_shapes=[
            pltpu.VMEM((table.shape[0], width), F32),
            pltpu.VMEM((slots * RAY_BLOCK, width), F32),
        ],
        compiler_params=pltpu.CompilerParams(vmem_limit_bytes=24 << 20),
        name="forward",
    )(space_at, cells, counts, order, table, mats, bias, density_head, cotangent)

    gathered = pack[None]
    step = 1
    while step < parts:
        other = lax.ppermute(gathered, "space", partners(parts, step))
        gathered = jnp.concatenate([gathered, other], axis=0)
        step *= 2

    piece_rows = width // ray_parts
    top_pieces, half, sums, shaded = pl.pallas_call(
        top_kernel,
        out_shape=(
            shape((ray_parts, 2 * piece_rows, width), F32),
            shape((rows, width), BF16),
            shape((8, width), F32),
            shape((rays, width), F32),
        ),
        in_specs=[SMEM] + [VMEM] * 11,
        out_specs=(VMEM,) * 4,
        scratch_shapes=[pltpu.VMEM((width, width), F32)] * 2,
        compiler_params=pltpu.CompilerParams(vmem_limit_bytes=24 << 20),
        name="top",
    )(ray_at, gathered, rel, counts, logit, side, cotangent, colour, density_head, mats, hidden, feats)

    top_got = [lax.ppermute(top_pieces[k], "ray", partners(ray_parts, k)) for k in range(1, ray_parts)]

    low_pieces = pl.pallas_call(
        low_kernel,
        out_shape=shape((ray_parts, 2 * piece_rows + 8, width), F32),
        in_specs=[SMEM] + [VMEM] * 4,
        out_specs=VMEM,
        scratch_shapes=[pltpu.VMEM((width, width), F32)] * 2 + [pltpu.VMEM((8, width), F32)],
        compiler_params=pltpu.CompilerParams(vmem_limit_bytes=24 << 20),
        name="low",
    )(ray_at, half, sums, mats, hidden)

    low_got = [lax.ppermute(low_pieces[k], "ray", partners(ray_parts, k)) for k in range(1, ray_parts)]

    top_own = top_pieces[0] + sum(top_got[1:], top_got[0])
    low_own = low_pieces[0] + sum(low_got[1:], low_got[0])
    small = low_own[2 * piece_rows :]
    low_own = low_own[: 2 * piece_rows]
    top_all = [top_own] + [lax.ppermute(top_own, "ray", partners(ray_parts, k)) for k in range(1, ray_parts)]
    low_all = [low_own] + [lax.ppermute(low_own, "ray", partners(ray_parts, k)) for k in range(1, ray_parts)]

    composite = shaded
    step = 1
    while step < parts:
        keep = (space // step) % 2
        halves = composite.reshape(parts // (2 * step), 2, -1, width)
        mine = lax.dynamic_index_in_dim(halves, keep, 1, keepdims=False)
        theirs = lax.dynamic_index_in_dim(halves, 1 - keep, 1, keepdims=False)
        composite = mine + lax.ppermute(theirs, "space", partners(parts, step))
        step *= 2
    composite = composite.reshape(-1, width)

    weight_grads = pl.pallas_call(
        join_kernel,
        out_shape=shape((layers, width, width), F32),
        in_specs=[SMEM] + [VMEM] * (2 * ray_parts),
        out_specs=VMEM,
        compiler_params=pltpu.CompilerParams(vmem_limit_bytes=8 << 20),
        name="join",
    )(ray_at, *top_all, *low_all)

    bias_grads = jnp.concatenate([small[4:5], small[3:4], small[2:3], small[0:1]], axis=0)
    return (composite, weight_grads[None], bias_grads[None], small[1:2])


def solution(mesh):
    placed = (
        P("space", None, None),
        P("space", None, None, None),
        P("space", None, None),
        P("space", None),
        P("space", "ray", None),
        P("ray", "space"),
        P("ray", None),
        P("ray", None),
    )
    return jax.shard_map(
        on_device,
        mesh=mesh,
        in_specs=placed,
        out_specs=(
            P(("ray", "space"), None),
            P("space", None, None, None),
            P("space", None, None),
            P("space", None),
        ),
        check_vma=False,
    )
```

```python
import functools

import jax
import jax.numpy as jnp
from jax import lax
from jax.experimental import pallas as pl
from jax.experimental.pallas import tpu as pltpu
from jax.sharding import PartitionSpec as P

step_length = 0.05
RAY_BLOCK = 128
GATHER_UNROLL = 64

F32 = jnp.float32
BF16 = jnp.bfloat16
VMEM = pl.BlockSpec(memory_space=pltpu.VMEM)
SMEM = pl.BlockSpec(memory_space=pltpu.SMEM)


def columns(rows, block):
    n = rows.shape[0]
    square = jnp.concatenate([rows, jnp.zeros((block - n, block), F32)], axis=0).T
    return [square[:, i : i + 1] for i in range(n)]


def row_block(cols, block):
    lane = lax.broadcasted_iota(jnp.int32, (block, block), 1)
    square = jnp.zeros((block, block), F32)
    for i, col in enumerate(cols):
        square = jnp.where(lane == i, col, square)
    return square.T[: len(cols)]


def before_of(optical):
    slots = optical.shape[0]
    place = lax.broadcasted_iota(jnp.int32, optical.shape, 0)
    total = jnp.zeros_like(optical)
    for j in range(slots - 1):
        total = total + jnp.where(place > j, optical[j : j + 1], 0.0)
    return total


def forward_kernel(
    space_ref, cells_ref, counts_ref, order_ref, table_ref, mats_ref, bias_ref, head_ref, cot_ref,
    hidden_ref, logit_ref, side_ref, pack_ref, rel_ref, colour_ref,
    wide_table, rows_ref,
):
    layers, width = bias_ref.shape
    parts, block = order_ref.shape
    span = hidden_ref.shape[1]
    slots = span // block
    half = width // 2
    cells_per = 256
    c = pl.program_id(0)

    @pl.when(c == 0)
    def _():
        @pl.loop(0, table_ref.shape[0] // cells_per)
        def _(t):
            at = pl.multiple_of(t * cells_per, cells_per)
            wide = table_ref[pl.ds(at, cells_per), :].astype(F32)
            for side in range(2):
                wide_table[pl.ds(2 * at + side, cells_per, stride=2), :] = wide[:, side * half : (side + 1) * half]

    @pl.loop(0, span // GATHER_UNROLL)
    def _(j):
        base = pl.multiple_of(j * GATHER_UNROLL, GATHER_UNROLL)
        for u in range(GATHER_UNROLL):
            cell = cells_ref[c * span + base + u]
            rows_ref[pl.ds(2 * base + 2 * u, 2), :] = wide_table[pl.ds(2 * cell, 2), :]

    me = space_ref[0]
    for k in range(parts):
        rel_ref[k : k + 1, :] = order_ref[pl.ds(me ^ k, 1), :]

    head = head_ref[...]
    hidden = jnp.concatenate(
        [rows_ref[pl.ds(side, span, stride=2), :].astype(BF16) for side in range(2)], axis=1
    )
    linear = None
    for layer in range(layers):
        hidden_ref[layer] = hidden
        linear = jnp.dot(hidden, mats_ref[layer], preferred_element_type=F32) + bias_ref[layer : layer + 1, :]
        if layer + 1 < layers:
            hidden = jnp.maximum(linear, 0.0).astype(BF16)
    cot = cot_ref[...]
    cols = []
    for i in range(slots):
        cols.append(jnp.sum(linear[i * block : (i + 1) * block] * head, axis=1, keepdims=True))
    for i in range(slots):
        cols.append(jnp.sum(linear[i * block : (i + 1) * block] * cot, axis=1, keepdims=True))
    both = row_block(cols, block)
    logit = both[:slots]
    side = both[slots:]
    density = jnp.maximum(logit, 0.0) + jnp.log1p(jnp.exp(-jnp.abs(logit)))
    place = lax.broadcasted_iota(jnp.int32, (slots, block), 0)
    live = place < counts_ref[...]
    optical = jnp.where(live, density * step_length, 0.0)
    blend = jnp.exp(-before_of(optical)) * (1.0 - jnp.exp(-optical))
    logit_ref[...] = logit
    side_ref[...] = side
    pack_ref[0:1, :] = -jnp.sum(optical, axis=0, keepdims=True)
    pack_ref[1:2, :] = jnp.sum(blend * side, axis=0, keepdims=True)
    colour = jnp.zeros((block, width), F32)
    for i, col in enumerate(columns(blend, block)):
        colour = colour + col * linear[i * block : (i + 1) * block]
    colour_ref[...] = colour


def layer_back(half, below, mats, layer):
    back = lax.dot_general(half, mats[layer], (((1,), (1,)), ((), ())), preferred_element_type=F32)
    return jnp.where(below > 0, back, 0.0)


def mat_grad(below, half):
    return lax.dot_general(below, half, (((0,), (0,)), ((), ())), preferred_element_type=F32)


def store_pieces(pieces_ref, slot, total, me):
    count = pieces_ref.shape[0]
    rows = total.shape[0] // count
    for owner in range(count):
        pieces_ref[pl.ds(owner ^ me, 1), slot * rows : (slot + 1) * rows, :] = total[owner * rows : (owner + 1) * rows][None]


def top_kernel(
    ray_ref, gathered_ref, rel_ref, counts_ref, logit_ref, side_ref, cot_ref, colour_ref, head_ref, bias_ref, mats_ref, hidden_ref,
    pieces_ref, half_ref, sums_ref, shaded_ref,
    acc_top, acc_next,
):
    layers = mats_ref.shape[0]
    top = layers - 1
    slots, block = logit_ref.shape
    parts = rel_ref.shape[0]
    width = head_ref.shape[1]
    head = head_ref[...]
    c = pl.program_id(0)

    @pl.when(c == 0)
    def _():
        acc_top[...] = jnp.zeros_like(acc_top)
        acc_next[...] = jnp.zeros_like(acc_next)
        sums_ref[...] = jnp.zeros_like(sums_ref)

    rank = rel_ref[...]
    decays = gathered_ref[:, 0, :]
    products = gathered_ref[:, 1, :]
    ahead = jnp.zeros((parts, block), F32)
    for q in range(parts):
        ahead = ahead + jnp.where(rank[q : q + 1] < rank, decays[q : q + 1], 0.0)
    prefixes = jnp.exp(ahead)
    share = prefixes * products
    tail = jnp.sum(jnp.where(rank > rank[0:1], share, 0.0), axis=0, keepdims=True)
    prefix = prefixes[0:1]

    logit = logit_ref[...]
    grown = jnp.exp(-jnp.abs(logit))
    density = jnp.maximum(logit, 0.0) + jnp.log1p(grown)
    slope = jnp.where(logit >= 0, 1.0, grown) / (1.0 + grown)
    place = lax.broadcasted_iota(jnp.int32, (slots, block), 0)
    live = place < counts_ref[...]
    optical = jnp.where(live, density * step_length, 0.0)
    reach = jnp.exp(-before_of(optical))
    passed = jnp.exp(-optical)
    blend = reach * (1.0 - passed)
    grad_blend = prefix * side_ref[...]
    lost = blend * grad_blend
    after = jnp.zeros_like(lost)
    for j in range(1, slots):
        after = after + jnp.where(place < j, lost[j : j + 1], 0.0)
    grad_optical = reach * passed * grad_blend - after - tail
    grad_logit = jnp.where(live, grad_optical * step_length, 0.0) * slope
    cols = columns(jnp.concatenate([blend * prefix, grad_logit, prefix, jnp.zeros((7, block), F32)], axis=0), block)
    cot = cot_ref[...]
    shaded_ref[...] = cols[2 * slots] * colour_ref[...]
    below = hidden_ref[1]
    grads = []
    head_sum = jnp.zeros((block, width), F32)
    bias_sum = jnp.zeros((block, width), F32)
    for i in range(slots):
        grad = cols[i] * cot + cols[slots + i] * head
        bias_sum = bias_sum + grad
        head_sum = head_sum + cols[slots + i] * below[i * block : (i + 1) * block].astype(F32)
        grads.append(grad.astype(BF16))
    logit_sum = jnp.sum(jnp.sum(grad_logit, axis=0, keepdims=True), axis=1, keepdims=True)
    sums_ref[0:1, :] += jnp.sum(bias_sum, axis=0, keepdims=True)
    sums_ref[1:2, :] += jnp.sum(head_sum, axis=0, keepdims=True)
    sums_ref[3:4, :] += jnp.broadcast_to(logit_sum, (1, width))
    half = jnp.concatenate(grads, axis=0)
    acc_top[...] += mat_grad(below, half)
    grad = layer_back(half, below, mats_ref, top)
    sums_ref[2:3, :] += jnp.sum(grad, axis=0, keepdims=True)
    half = grad.astype(BF16)
    half_ref[...] = half
    acc_next[...] += mat_grad(hidden_ref[0], half)

    @pl.when(c == pl.num_programs(0) - 1)
    def _():
        me = ray_ref[0]
        store_pieces(pieces_ref, 0, acc_top[...], me)
        store_pieces(pieces_ref, 1, acc_next[...], me)
        mixed = jnp.dot(
            sums_ref[...], mats_ref[top].astype(F32), precision=lax.Precision.HIGHEST, preferred_element_type=F32
        )
        sums_ref[1:2, :] = mixed[1:2, :] + sums_ref[3:4, :] * bias_ref[top : top + 1, :]


def low_kernel(ray_ref, half_ref, sums_ref, mats_ref, hidden_ref, pieces_ref, acc_a, acc_b, bias_ref):
    c = pl.program_id(0)

    @pl.when(c == 0)
    def _():
        acc_a[...] = jnp.zeros_like(acc_a)
        acc_b[...] = jnp.zeros_like(acc_b)
        bias_ref[...] = jnp.zeros_like(bias_ref)

    grad = layer_back(half_ref[...], hidden_ref[2], mats_ref, 2)
    bias_ref[0:1, :] += jnp.sum(grad, axis=0, keepdims=True)
    half = grad.astype(BF16)
    below = hidden_ref[1]
    acc_a[...] += mat_grad(below, half)
    grad = layer_back(half, below, mats_ref, 1)
    bias_ref[1:2, :] += jnp.sum(grad, axis=0, keepdims=True)
    half = grad.astype(BF16)
    acc_b[...] += mat_grad(hidden_ref[0], half)

    @pl.when(c == pl.num_programs(0) - 1)
    def _():
        me = ray_ref[0]
        store_pieces(pieces_ref, 0, acc_a[...], me)
        store_pieces(pieces_ref, 1, acc_b[...], me)
        count = pieces_ref.shape[0]
        first = 2 * (acc_a.shape[0] // count)
        small = jnp.concatenate(
            [sums_ref[0:3, :], bias_ref[0:2, :], jnp.zeros((3, acc_a.shape[1]), F32)], axis=0
        )
        for k in range(count):
            pieces_ref[k, first : first + 8, :] = small


def join_kernel(ray_ref, *refs):
    *pieces, out_ref = refs
    me = ray_ref[0]
    layers, width = out_ref.shape[:2]
    count = len(pieces) // 2
    rows = width // count
    for chunk in range(2):
        for k in range(count):
            piece = pieces[chunk * count + k]
            at = pl.ds(pl.multiple_of((me ^ k) * rows, rows), rows)
            for slot in range(2):
                out_ref[layers - 1 - 2 * chunk - slot, at, :] = piece[slot * rows : (slot + 1) * rows, :]


def partners(count, k):
    return [(i, i ^ k) for i in range(count)]


def on_device(
    grid_table, weights, biases, density_head, sample_cells, sample_counts, ray_order, cotangent
):
    table = grid_table[0]
    mats = weights[0]
    bias = biases[0]
    slots = sample_cells.shape[2]
    cells = sample_cells[0].T.reshape(slots, -1, RAY_BLOCK).transpose(1, 0, 2).reshape(-1)
    counts = sample_counts.T
    order = ray_order.T
    space = lax.axis_index("space")
    ray = lax.axis_index("ray")
    parts = lax.axis_size("space")
    ray_parts = lax.axis_size("ray")
    space_at = space.astype(jnp.int32)[None]
    ray_at = ray.astype(jnp.int32)[None]
    layers, width = bias.shape
    rays = sample_cells.shape[1]
    rows = slots * rays
    shape = jax.ShapeDtypeStruct

    block = RAY_BLOCK
    steps = rays // block
    span = slots * block

    def whole(*dims):
        return pl.BlockSpec(dims, lambda c: (0,) * len(dims), pipeline_mode=pl.Buffered(1))

    def result(*dims):
        return pl.BlockSpec(dims, lambda c: (0,) * len(dims))

    def per_ray(count):
        return pl.BlockSpec((count, block), lambda c: (0, c))

    ray_rows = pl.BlockSpec((block, width), lambda c: (c, 0))

    hidden, logit, side, pack, rel, colour = pl.pallas_call(
        forward_kernel,
        grid=(steps,),
        out_shape=(
            shape((layers, rows, width), BF16),
            shape((slots, rays), F32),
            shape((slots, rays), F32),
            shape((2, rays), F32),
            shape((parts, rays), jnp.int32),
            shape((rays, width), F32),
        ),
        in_specs=[
            SMEM, SMEM, per_ray(1), per_ray(parts), whole(*table.shape), whole(*mats.shape), whole(*bias.shape),
            whole(1, width), ray_rows,
        ],
        out_specs=(
            pl.BlockSpec((layers, span, width), lambda c: (0, c, 0)),
            per_ray(slots), per_ray(slots), per_ray(2), per_ray(parts), ray_rows,
        ),
        scratch_shapes=[
            pltpu.VMEM((2 * table.shape[0], width // 2), F32),
            pltpu.VMEM((2 * span, width // 2), F32),
        ],
        name="forward",
    )(space_at, cells, counts, order, table, mats, bias, density_head, cotangent)

    gathered = pack[None]
    step = 1
    while step < parts:
        other = lax.ppermute(gathered, "space", partners(parts, step))
        gathered = jnp.concatenate([gathered, other], axis=0)
        step *= 2

    piece_rows = width // ray_parts
    top_pieces, half, sums, shaded = pl.pallas_call(
        top_kernel,
        grid=(steps,),
        out_shape=(
            shape((ray_parts, 2 * piece_rows, width), F32),
            shape((rows, width), BF16),
            shape((8, width), F32),
            shape((rays, width), F32),
        ),
        in_specs=[
            SMEM, pl.BlockSpec((parts, 2, block), lambda c: (0, 0, c)), per_ray(parts), per_ray(1), per_ray(slots),
            per_ray(slots), ray_rows, ray_rows, whole(1, width), whole(*bias.shape), whole(*mats.shape),
            pl.BlockSpec((2, span, width), lambda c: (layers // 2 - 1, c, 0)),
        ],
        out_specs=(
            result(ray_parts, 2 * piece_rows, width),
            pl.BlockSpec((span, width), lambda c: (c, 0)),
            result(8, width),
            ray_rows,
        ),
        scratch_shapes=[pltpu.VMEM((width, width), F32)] * 2,
        name="top",
    )(ray_at, gathered, rel, counts, logit, side, cotangent, colour, density_head, bias, mats, hidden)

    top_got = [lax.ppermute(top_pieces[k], "ray", partners(ray_parts, k)) for k in range(1, ray_parts)]

    low_pieces = pl.pallas_call(
        low_kernel,
        grid=(steps,),
        out_shape=shape((ray_parts, 2 * piece_rows + 8, width), F32),
        in_specs=[
            SMEM, pl.BlockSpec((span, width), lambda c: (c, 0)), whole(8, width), whole(*mats.shape),
            pl.BlockSpec((3, span, width), lambda c: (0, c, 0)),
        ],
        out_specs=result(ray_parts, 2 * piece_rows + 8, width),
        scratch_shapes=[pltpu.VMEM((width, width), F32)] * 2 + [pltpu.VMEM((8, width), F32)],
        name="low",
    )(ray_at, half, sums, mats, hidden)

    low_got = [lax.ppermute(low_pieces[k], "ray", partners(ray_parts, k)) for k in range(1, ray_parts)]

    top_own = top_pieces[0] + sum(top_got[1:], top_got[0])
    low_own = low_pieces[0] + sum(low_got[1:], low_got[0])
    small = low_own[2 * piece_rows :]
    low_own = low_own[: 2 * piece_rows]
    top_all = [top_own] + [lax.ppermute(top_own, "ray", partners(ray_parts, k)) for k in range(1, ray_parts)]
    low_all = [low_own] + [lax.ppermute(low_own, "ray", partners(ray_parts, k)) for k in range(1, ray_parts)]

    composite = shaded
    step = 1
    while step < parts:
        keep = (space // step) % 2
        halves = composite.reshape(parts // (2 * step), 2, -1, width)
        mine = lax.dynamic_index_in_dim(halves, keep, 1, keepdims=False)
        theirs = lax.dynamic_index_in_dim(halves, 1 - keep, 1, keepdims=False)
        composite = mine + lax.ppermute(theirs, "space", partners(parts, step))
        step *= 2
    composite = composite.reshape(-1, width)

    weight_grads = pl.pallas_call(
        join_kernel,
        out_shape=shape((layers, width, width), F32),
        in_specs=[SMEM] + [VMEM] * (2 * ray_parts),
        out_specs=VMEM,
        compiler_params=pltpu.CompilerParams(vmem_limit_bytes=8 << 20),
        name="join",
    )(ray_at, *top_all, *low_all)

    bias_grads = jnp.concatenate([small[4:5], small[3:4], small[2:3], small[0:1]], axis=0)
    return (composite, weight_grads[None], bias_grads[None], small[1:2])


def solution(mesh):
    placed = (
        P("space", None, None),
        P("space", None, None, None),
        P("space", None, None),
        P("space", None),
        P("space", "ray", None),
        P("ray", "space"),
        P("ray", None),
        P("ray", None),
    )
    return jax.shard_map(
        on_device,
        mesh=mesh,
        in_specs=placed,
        out_specs=(
            P(("ray", "space"), None),
            P("space", None, None, None),
            P("space", None, None),
            P("space", None),
        ),
        check_vma=False,
    )
```

```python
import functools

import jax
import jax.numpy as jnp
from jax import lax
from jax.experimental import pallas as pl
from jax.experimental.pallas import tpu as pltpu
from jax.sharding import PartitionSpec as P

step_length = 0.05
RAY_BLOCK = 128
GATHER_UNROLL = 64
LOW_SPAN = 1024
GRANT = 20 << 20

F32 = jnp.float32
BF16 = jnp.bfloat16
VMEM = pl.BlockSpec(memory_space=pltpu.VMEM)
SMEM = pl.BlockSpec(memory_space=pltpu.SMEM)
HBM = pl.BlockSpec(memory_space=pltpu.HBM)


def columns(rows, block):
    n = rows.shape[0]
    square = jnp.concatenate([rows, jnp.zeros((block - n, block), F32)], axis=0).T
    return [square[:, i : i + 1] for i in range(n)]


def row_block(cols, block):
    lane = lax.broadcasted_iota(jnp.int32, (block, block), 1)
    square = jnp.zeros((block, block), F32)
    for i, col in enumerate(cols):
        square = jnp.where(lane == i, col, square)
    return square.T[: len(cols)]


def before_of(optical):
    slots = optical.shape[0]
    place = lax.broadcasted_iota(jnp.int32, optical.shape, 0)
    total = jnp.zeros_like(optical)
    for j in range(slots - 1):
        total = total + jnp.where(place > j, optical[j : j + 1], 0.0)
    return total


def forward_kernel(
    cells_hbm, counts_hbm, order_hbm, table_hbm, mats_hbm, bias_hbm, head_hbm, cot_hbm,
    hidden_ref, logit_ref, side_ref, pack_ref, rel_ref, colour_ref, counts_ref, mats_ref, bias_ref, head_ref, cot_ref,
    cells_ref, order_ref, table_ref, wide_table, rows_ref, small_sem, table_sem,
):
    layers, width = bias_ref.shape
    parts, rays = order_ref.shape
    block = RAY_BLOCK
    span = rows_ref.shape[0] // 2
    slots = span // block
    half = width // 2
    cells = table_ref.shape[0]
    pieces = table_sem.shape[0]
    piece = cells // pieces
    cells_per = 256

    table_copies = []
    for t in range(pieces):
        at = pl.ds(t * piece, piece)
        table_copies.append(pltpu.make_async_copy(table_hbm.at[at], table_ref.at[at], table_sem.at[t]))
        table_copies[-1].start()
    copies = []
    pairs = (
        (order_hbm, order_ref), (mats_hbm, mats_ref), (bias_hbm, bias_ref), (head_hbm, head_ref), (cot_hbm, cot_ref),
        (counts_hbm, counts_ref), (cells_hbm, cells_ref),
    )
    for t, (source, target) in enumerate(pairs):
        copies.append(pltpu.make_async_copy(source, target, small_sem.at[t]))
        copies[-1].start()

    for t in range(pieces):
        table_copies[t].wait()

        @pl.loop(0, piece // cells_per)
        def _(n):
            at = pl.multiple_of(t * piece + n * cells_per, cells_per)
            wide = table_ref[pl.ds(at, cells_per), :].astype(F32)
            for side in range(2):
                wide_table[pl.ds(2 * at + side, cells_per, stride=2), :] = wide[:, side * half : (side + 1) * half]

    copies.pop().wait()

    def gather(first, base, count):
        for u in range(count):
            cell = cells_ref[first + base + u]
            rows_ref[pl.ds(2 * base + 2 * u, 2), :] = wide_table[pl.ds(2 * cell, 2), :]

    @pl.loop(0, span // GATHER_UNROLL)
    def _(j):
        gather(0, pl.multiple_of(j * GATHER_UNROLL, GATHER_UNROLL), GATHER_UNROLL)

    for copy in copies:
        copy.wait()
    me = lax.axis_index("space")
    for k in range(parts):
        rel_ref[k : k + 1, :] = order_ref[pl.ds(me ^ k, 1), :]

    def compute(c, more):
        at = pl.ds(pl.multiple_of(c * span, span), span)
        ray_at = pl.ds(pl.multiple_of(c * block, block), block)
        head = head_ref[...]
        hidden = jnp.concatenate(
            [rows_ref[pl.ds(side, span, stride=2), :].astype(BF16) for side in range(2)], axis=1
        )
        if more:
            gather((c + 1) * span, 0, span)
        linear = None
        for layer in range(layers):
            hidden_ref[layer, at, :] = hidden
            linear = jnp.dot(hidden, mats_ref[layer], preferred_element_type=F32) + bias_ref[layer : layer + 1, :]
            if layer + 1 < layers:
                hidden = jnp.maximum(linear, 0.0).astype(BF16)
        cot = cot_ref[ray_at, :]
        cols = []
        for i in range(slots):
            cols.append(jnp.sum(linear[i * block : (i + 1) * block] * head, axis=1, keepdims=True))
        for i in range(slots):
            cols.append(jnp.sum(linear[i * block : (i + 1) * block] * cot, axis=1, keepdims=True))
        both = row_block(cols, block)
        logit = both[:slots]
        side = both[slots:]
        density = jnp.maximum(logit, 0.0) + jnp.log1p(jnp.exp(-jnp.abs(logit)))
        place = lax.broadcasted_iota(jnp.int32, (slots, block), 0)
        live = place < counts_ref[:, ray_at]
        optical = jnp.where(live, density * step_length, 0.0)
        blend = jnp.exp(-before_of(optical)) * (1.0 - jnp.exp(-optical))
        logit_ref[:, ray_at] = logit
        side_ref[:, ray_at] = side
        pack_ref[0:1, ray_at] = -jnp.sum(optical, axis=0, keepdims=True)
        pack_ref[1:2, ray_at] = jnp.sum(blend * side, axis=0, keepdims=True)
        colour = jnp.zeros((block, width), F32)
        for i, col in enumerate(columns(blend, block)):
            colour = colour + col * linear[i * block : (i + 1) * block]
        colour_ref[ray_at, :] = colour

    steps = rays // block

    @pl.loop(0, steps - 1)
    def _(c):
        compute(c, True)

    compute(steps - 1, False)


def layer_back(half, below, mats, layer):
    back = lax.dot_general(half, mats[layer], (((1,), (1,)), ((), ())), preferred_element_type=F32)
    return jnp.where(below > 0, back, 0.0)


def mat_grad(below, half):
    return lax.dot_general(below, half, (((0,), (0,)), ((), ())), preferred_element_type=F32)


def store_pieces(pieces_ref, slot, total, me):
    count = pieces_ref.shape[0]
    rows = total.shape[0] // count
    for owner in range(count):
        pieces_ref[pl.ds(owner ^ me, 1), slot * rows : (slot + 1) * rows, :] = total[owner * rows : (owner + 1) * rows][None]


def top_kernel(
    gathered_ref, rel_ref, counts_ref, logit_ref, side_ref, cot_ref, colour_ref, head_ref, bias_ref, mats_ref, hidden_ref,
    pieces_ref, half_ref, sums_ref, shaded_ref,
    acc_top, acc_next,
):
    layers = mats_ref.shape[0]
    top = layers - 1
    slots, rays = logit_ref.shape
    parts = rel_ref.shape[0]
    width = head_ref.shape[1]
    block = RAY_BLOCK
    span = slots * block
    head = head_ref[...]
    space = lax.axis_index("space")
    per = rays // parts
    acc_top[...] = jnp.zeros_like(acc_top)
    acc_next[...] = jnp.zeros_like(acc_next)
    sums_ref[...] = jnp.zeros_like(sums_ref)

    @pl.loop(0, rays // block)
    def _(c):
        at = pl.ds(pl.multiple_of(c * span, span), span)
        ray_at = pl.ds(pl.multiple_of(c * block, block), block)
        rank = rel_ref[:, ray_at]
        decays = gathered_ref[:, 0, ray_at]
        products = gathered_ref[:, 1, ray_at]
        ahead = jnp.zeros((parts, block), F32)
        for q in range(parts):
            ahead = ahead + jnp.where(rank[q : q + 1] < rank, decays[q : q + 1], 0.0)
        prefixes = jnp.exp(ahead)
        share = prefixes * products
        tail = jnp.sum(jnp.where(rank > rank[0:1], share, 0.0), axis=0, keepdims=True)
        prefix = prefixes[0:1]

        logit = logit_ref[:, ray_at]
        grown = jnp.exp(-jnp.abs(logit))
        density = jnp.maximum(logit, 0.0) + jnp.log1p(grown)
        slope = jnp.where(logit >= 0, 1.0, grown) / (1.0 + grown)
        place = lax.broadcasted_iota(jnp.int32, (slots, block), 0)
        live = place < counts_ref[:, ray_at]
        optical = jnp.where(live, density * step_length, 0.0)
        reach = jnp.exp(-before_of(optical))
        passed = jnp.exp(-optical)
        blend = reach * (1.0 - passed)
        grad_blend = prefix * side_ref[:, ray_at]
        lost = blend * grad_blend
        after = jnp.zeros_like(lost)
        for j in range(1, slots):
            after = after + jnp.where(place < j, lost[j : j + 1], 0.0)
        grad_optical = reach * passed * grad_blend - after - tail
        grad_logit = jnp.where(live, grad_optical * step_length, 0.0) * slope
        cols = columns(jnp.concatenate([blend * prefix, grad_logit, prefix, jnp.zeros((7, block), F32)], axis=0), block)
        cot = cot_ref[ray_at, :]
        shaded = cols[2 * slots] * colour_ref[ray_at, :]
        for n in range(block // per):
            owner = c * (block // per) + n
            shaded_ref[pl.ds((owner ^ space) & 1, 1), pl.ds(owner >> 1, 1)] = shaded[n * per : (n + 1) * per][None, None]
        below = hidden_ref[top, at, :]
        grads = []
        head_sum = jnp.zeros((block, width), F32)
        bias_sum = jnp.zeros((block, width), F32)
        for i in range(slots):
            grad = cols[i] * cot + cols[slots + i] * head
            bias_sum = bias_sum + grad
            head_sum = head_sum + cols[slots + i] * below[i * block : (i + 1) * block].astype(F32)
            grads.append(grad.astype(BF16))
        logit_sum = jnp.sum(jnp.sum(grad_logit, axis=0, keepdims=True), axis=1, keepdims=True)
        sums_ref[0:1, :] += jnp.sum(bias_sum, axis=0, keepdims=True)
        sums_ref[1:2, :] += jnp.sum(head_sum, axis=0, keepdims=True)
        sums_ref[3:4, :] += jnp.broadcast_to(logit_sum, (1, width))
        half = jnp.concatenate(grads, axis=0)
        acc_top[...] += mat_grad(below, half)
        grad = layer_back(half, below, mats_ref, top)
        sums_ref[2:3, :] += jnp.sum(grad, axis=0, keepdims=True)
        half = grad.astype(BF16)
        half_ref[at, :] = half
        acc_next[...] += mat_grad(hidden_ref[top - 1, at, :], half)

    me = lax.axis_index("ray")
    store_pieces(pieces_ref, 0, acc_top[...], me)
    store_pieces(pieces_ref, 1, acc_next[...], me)
    mixed = jnp.dot(
        sums_ref[...], mats_ref[top].astype(F32), precision=lax.Precision.HIGHEST, preferred_element_type=F32
    )
    sums_ref[1:2, :] = mixed[1:2, :] + sums_ref[3:4, :] * bias_ref[top : top + 1, :]


def low_kernel(half_ref, sums_ref, mats_ref, hidden_ref, pieces_ref, acc_a, acc_b, bias_ref):
    rows = half_ref.shape[0]
    span = LOW_SPAN
    acc_a[...] = jnp.zeros_like(acc_a)
    acc_b[...] = jnp.zeros_like(acc_b)
    bias_ref[...] = jnp.zeros_like(bias_ref)

    @pl.loop(0, rows // span)
    def _(c):
        at = pl.ds(pl.multiple_of(c * span, span), span)
        grad = layer_back(half_ref[at, :], hidden_ref[2, at, :], mats_ref, 2)
        bias_ref[0:1, :] += jnp.sum(grad, axis=0, keepdims=True)
        half = grad.astype(BF16)
        below = hidden_ref[1, at, :]
        acc_a[...] += mat_grad(below, half)
        grad = layer_back(half, below, mats_ref, 1)
        bias_ref[1:2, :] += jnp.sum(grad, axis=0, keepdims=True)
        half = grad.astype(BF16)
        acc_b[...] += mat_grad(hidden_ref[0, at, :], half)

    me = lax.axis_index("ray")
    store_pieces(pieces_ref, 0, acc_a[...], me)
    store_pieces(pieces_ref, 1, acc_b[...], me)
    count = pieces_ref.shape[0]
    first = 2 * (acc_a.shape[0] // count)
    small = jnp.concatenate(
        [sums_ref[0:3, :], bias_ref[0:2, :], jnp.zeros((3, acc_a.shape[1]), F32)], axis=0
    )
    for k in range(count):
        pieces_ref[k, first : first + 8, :] = small


def fold_kernel(step, kept_ref, other_ref, out_ref):
    bit = (lax.axis_index("space") // step) & 1
    for j in range(other_ref.shape[0]):
        out_ref[pl.ds((j & 1) ^ bit, 1), j >> 1] = (kept_ref[0, j] + other_ref[j])[None]


def join_kernel(*refs):
    *inputs, small_ref, kept_ref, other_ref, out_ref, bias_ref, head_ref, composite_ref = refs
    me = lax.axis_index("ray")
    layers, width = out_ref.shape[:2]
    count = len(inputs) // 2
    rows = width // count
    for chunk in range(2):
        for k in range(count):
            piece = inputs[chunk * count + k]
            at = pl.ds(pl.multiple_of((me ^ k) * rows, rows), rows)
            for slot in range(2):
                out_ref[layers - 1 - 2 * chunk - slot, at, :] = piece[slot * rows : (slot + 1) * rows, :]
    first = 2 * rows
    bias_ref[...] = jnp.concatenate(
        [small_ref[first + n : first + n + 1, :] for n in (4, 3, 2, 0)], axis=0
    )
    head_ref[...] = small_ref[first + 1 : first + 2, :]
    composite_ref[...] = kept_ref[0, 0] + other_ref[0]


def partners(count, k):
    return [(i, i ^ k) for i in range(count)]


def on_device(
    grid_table, weights, biases, density_head, sample_cells, sample_counts, ray_order, cotangent
):
    table = grid_table[0]
    mats = weights[0]
    bias = biases[0]
    slots = sample_cells.shape[2]
    cells = sample_cells[0].T.reshape(slots, -1, RAY_BLOCK).transpose(1, 0, 2).reshape(-1)
    counts = sample_counts.T
    order = ray_order.T
    parts = lax.axis_size("space")
    ray_parts = lax.axis_size("ray")
    layers, width = bias.shape
    rays = sample_cells.shape[1]
    rows = slots * rays
    span = slots * RAY_BLOCK
    shape = jax.ShapeDtypeStruct
    grant = pltpu.CompilerParams(vmem_limit_bytes=GRANT)

    inputs = (cells, counts, order, table, mats, bias, density_head, cotangent)
    hidden, logit, side, pack, rel, colour, counts, mats, bias, head, cot = pl.pallas_call(
        forward_kernel,
        out_shape=(
            shape((layers, rows, width), BF16),
            shape((slots, rays), F32),
            shape((slots, rays), F32),
            shape((2, rays), F32),
            shape((parts, rays), jnp.int32),
            shape((rays, width), F32),
            shape(counts.shape, jnp.int32),
            shape(mats.shape, BF16),
            shape(bias.shape, F32),
            shape(density_head.shape, F32),
            shape(cotangent.shape, F32),
        ),
        in_specs=[HBM] * 8,
        out_specs=(VMEM,) * 11,
        scratch_shapes=[
            pltpu.SMEM(cells.shape, jnp.int32),
            pltpu.VMEM((parts, rays), jnp.int32),
            pltpu.VMEM(table.shape, BF16),
            pltpu.VMEM((2 * table.shape[0], width // 2), F32),
            pltpu.VMEM((2 * span, width // 2), F32),
            pltpu.SemaphoreType.DMA((7,)),
            pltpu.SemaphoreType.DMA((4,)),
        ],
        compiler_params=grant,
        name="forward",
    )(*[pltpu.with_memory_space_constraint(x, pltpu.HBM) for x in inputs])

    gathered = pack[None]
    step = 1
    while step < parts:
        other = lax.ppermute(gathered, "space", partners(parts, step))
        gathered = jnp.concatenate([gathered, other], axis=0)
        step *= 2

    piece_rows = width // ray_parts
    top_pieces, half, sums, shaded = pl.pallas_call(
        top_kernel,
        out_shape=(
            shape((ray_parts, 2 * piece_rows, width), F32),
            shape((rows, width), BF16),
            shape((8, width), F32),
            shape((2, parts // 2, rays // parts, width), F32),
        ),
        in_specs=[VMEM] * 11,
        out_specs=(VMEM,) * 4,
        scratch_shapes=[pltpu.VMEM((width, width), F32)] * 2,
        compiler_params=grant,
        name="top",
    )(gathered, rel, counts, logit, side, cot, colour, head, bias, mats, hidden)

    def shift(array, axis, count, k):
        return lax.ppermute(array, axis, partners(count, k))

    top_got = [shift(top_pieces[k], "ray", ray_parts, k) for k in range(1, ray_parts)]

    low_pieces = pl.pallas_call(
        low_kernel,
        out_shape=shape((ray_parts, 2 * piece_rows + 8, width), F32),
        in_specs=[VMEM] * 4,
        out_specs=VMEM,
        scratch_shapes=[pltpu.VMEM((width, width), F32)] * 2 + [pltpu.VMEM((8, width), F32)],
        compiler_params=grant,
        name="low",
    )(half, sums, mats, hidden)

    low_got = [shift(low_pieces[k], "ray", ray_parts, k) for k in range(1, ray_parts)]

    top_own = top_pieces[0] + sum(top_got[1:], top_got[0])
    low_own = low_pieces[0] + sum(low_got[1:], low_got[0])
    small = low_own
    low_own = low_own[: 2 * piece_rows]
    top_all = [top_own] + [shift(top_own, "ray", ray_parts, k) for k in range(1, ray_parts)]
    low_all = [low_own] + [shift(low_own, "ray", ray_parts, k) for k in range(1, ray_parts)]

    step = 1
    other = shift(shaded[1], "space", parts, step)
    while 2 * step < parts:
        step *= 2
        count, per = other.shape[0], other.shape[1]
        shaded = pl.pallas_call(
            functools.partial(fold_kernel, step),
            out_shape=shape((2, count // 2, per, width), F32),
            in_specs=[VMEM] * 2,
            out_specs=VMEM,
            compiler_params=pltpu.CompilerParams(vmem_limit_bytes=4 << 20),
            name="fold",
        )(shaded, other)
        other = shift(shaded[1], "space", parts, step)

    weight_grads, bias_grads, head_grads, composite = pl.pallas_call(
        join_kernel,
        out_shape=(
            shape((layers, width, width), F32),
            shape((layers, width), F32),
            shape((1, width), F32),
            shape((rays // parts, width), F32),
        ),
        in_specs=[VMEM] * (2 * ray_parts + 3),
        out_specs=(VMEM,) * 4,
        compiler_params=pltpu.CompilerParams(vmem_limit_bytes=8 << 20),
        name="join",
    )(*top_all, *low_all, small, shaded, other)

    return (composite, weight_grads[None], bias_grads[None], head_grads)


def solution(mesh):
    placed = (
        P("space", None, None),
        P("space", None, None, None),
        P("space", None, None),
        P("space", None),
        P("space", "ray", None),
        P("ray", "space"),
        P("ray", None),
        P("ray", None),
    )
    return jax.shard_map(
        on_device,
        mesh=mesh,
        in_specs=placed,
        out_specs=(
            P(("ray", "space"), None),
            P("space", None, None, None),
            P("space", None, None),
            P("space", None),
        ),
        check_vma=False,
    )
```

```python
import functools

import jax
import jax.numpy as jnp
from jax import lax
from jax.experimental import pallas as pl
from jax.experimental.pallas import tpu as pltpu
from jax.sharding import PartitionSpec as P

step_length = 0.05
RAY_BLOCK = 128
GATHER_UNROLL = 64
LOW_SPAN = 1024
GRANT = 20 << 20

F32 = jnp.float32
BF16 = jnp.bfloat16
VMEM = pl.BlockSpec(memory_space=pltpu.VMEM)
SMEM = pl.BlockSpec(memory_space=pltpu.SMEM)
HBM = pl.BlockSpec(memory_space=pltpu.HBM)


def columns(rows, block):
    n = rows.shape[0]
    square = jnp.concatenate([rows, jnp.zeros((block - n, block), F32)], axis=0).T
    return [square[:, i : i + 1] for i in range(n)]


def row_block(cols, block):
    lane = lax.broadcasted_iota(jnp.int32, (block, block), 1)
    square = jnp.zeros((block, block), F32)
    for i, col in enumerate(cols):
        square = jnp.where(lane == i, col, square)
    return square.T[: len(cols)]


def before_of(optical):
    slots = optical.shape[0]
    place = lax.broadcasted_iota(jnp.int32, optical.shape, 0)
    total = jnp.zeros_like(optical)
    for j in range(slots - 1):
        total = total + jnp.where(place > j, optical[j : j + 1], 0.0)
    return total


def forward_kernel(
    cells_hbm, counts_hbm, order_hbm, table_hbm, mats_hbm, bias_hbm, head_hbm, cot_hbm,
    hidden_ref, logit_ref, side_ref, pack_ref, rel_ref, colour_ref, counts_ref, mats_ref, bias_ref, head_ref, cot_ref,
    cells_ref, cells_vmem, order_ref, table_ref, wide_table, rows_ref, small_sem, table_sem, cell_sem,
):
    layers, width = bias_ref.shape
    parts, rays = order_ref.shape
    block = RAY_BLOCK
    span = rows_ref.shape[0] // 2
    slots = span // block
    half = width // 2
    cells = table_ref.shape[0]
    pieces = table_sem.shape[0]
    piece = cells // pieces
    cells_per = 256

    fetch = pltpu.make_async_copy(cells_hbm, cells_vmem, cell_sem.at[0])
    fetch.start()
    table_copies = []
    for t in range(pieces):
        at = pl.ds(t * piece, piece)
        table_copies.append(pltpu.make_async_copy(table_hbm.at[at], table_ref.at[at], table_sem.at[t]))
        table_copies[-1].start()
    copies = []
    pairs = (
        (order_hbm, order_ref), (mats_hbm, mats_ref), (bias_hbm, bias_ref), (head_hbm, head_ref), (cot_hbm, cot_ref),
        (counts_hbm, counts_ref),
    )
    for t, (source, target) in enumerate(pairs):
        copies.append(pltpu.make_async_copy(source, target, small_sem.at[t]))
        copies[-1].start()

    fetch.wait()
    cells_vmem[...] = cells_vmem[...] * 2
    settle = pltpu.make_async_copy(cells_vmem, cells_ref, cell_sem.at[1])
    settle.start()
    for t in range(pieces):
        table_copies[t].wait()

        @pl.loop(0, piece // cells_per)
        def _(n):
            at = pl.multiple_of(t * piece + n * cells_per, cells_per)
            wide = table_ref[pl.ds(at, cells_per), :].astype(F32)
            for side in range(2):
                wide_table[pl.ds(2 * at + side, cells_per, stride=2), :] = wide[:, side * half : (side + 1) * half]

    settle.wait()

    def gather(first, count):
        for u in range(count):
            at = first + u
            rows_ref[2 * u : 2 * u + 2, :] = wide_table[pl.ds(cells_ref[at // block, at % block], 2), :]

    gather(0, span)
    for copy in copies:
        copy.wait()
    me = lax.axis_index("space")
    for k in range(parts):
        rel_ref[k : k + 1, :] = order_ref[pl.ds(me ^ k, 1), :]

    def compute(c, more):
        at = pl.ds(c * span, span)
        ray_at = pl.ds(c * block, block)
        head = head_ref[...]
        hidden = jnp.concatenate(
            [rows_ref[pl.ds(side, span, stride=2), :].astype(BF16) for side in range(2)], axis=1
        )
        if more:
            gather((c + 1) * span, span)
        linear = None
        for layer in range(layers):
            hidden_ref[layer, at, :] = hidden
            linear = jnp.dot(hidden, mats_ref[layer], preferred_element_type=F32) + bias_ref[layer : layer + 1, :]
            if layer + 1 < layers:
                hidden = jnp.maximum(linear, 0.0).astype(BF16)
        cot = cot_ref[ray_at, :]
        cols = []
        for i in range(slots):
            cols.append(jnp.sum(linear[i * block : (i + 1) * block] * head, axis=1, keepdims=True))
        for i in range(slots):
            cols.append(jnp.sum(linear[i * block : (i + 1) * block] * cot, axis=1, keepdims=True))
        both = row_block(cols, block)
        logit = both[:slots]
        side = both[slots:]
        density = jnp.maximum(logit, 0.0) + jnp.log1p(jnp.exp(-jnp.abs(logit)))
        place = lax.broadcasted_iota(jnp.int32, (slots, block), 0)
        live = place < counts_ref[:, ray_at]
        optical = jnp.where(live, density * step_length, 0.0)
        blend = jnp.exp(-before_of(optical)) * (1.0 - jnp.exp(-optical))
        logit_ref[:, ray_at] = logit
        side_ref[:, ray_at] = side
        pack_ref[0:1, ray_at] = -jnp.sum(optical, axis=0, keepdims=True)
        pack_ref[1:2, ray_at] = jnp.sum(blend * side, axis=0, keepdims=True)
        colour = jnp.zeros((block, width), F32)
        for i, col in enumerate(columns(blend, block)):
            colour = colour + col * linear[i * block : (i + 1) * block]
        colour_ref[ray_at, :] = colour

    steps = rays // block

    for c in range(steps):
        compute(c, c + 1 < steps)


def layer_back(half, below, mats, layer):
    back = lax.dot_general(half, mats[layer], (((1,), (1,)), ((), ())), preferred_element_type=F32)
    return jnp.where(below > 0, back, 0.0)


def mat_grad(below, half):
    return lax.dot_general(below, half, (((0,), (0,)), ((), ())), preferred_element_type=F32)


def store_pieces(pieces_ref, slot, total, me):
    count = pieces_ref.shape[0]
    rows = total.shape[0] // count
    for owner in range(count):
        pieces_ref[pl.ds(owner ^ me, 1), slot * rows : (slot + 1) * rows, :] = total[owner * rows : (owner + 1) * rows][None]


def top_kernel(
    gathered_ref, rel_ref, counts_ref, logit_ref, side_ref, cot_ref, colour_ref, head_ref, bias_ref, mats_ref, hidden_ref,
    pieces_ref, half_ref, sums_ref, shaded_ref,
    acc_top, acc_next,
):
    layers = mats_ref.shape[0]
    top = layers - 1
    slots, rays = logit_ref.shape
    parts = rel_ref.shape[0]
    width = head_ref.shape[1]
    block = RAY_BLOCK
    span = slots * block
    head = head_ref[...]
    space = lax.axis_index("space")
    per = rays // parts
    acc_top[...] = jnp.zeros_like(acc_top)
    acc_next[...] = jnp.zeros_like(acc_next)
    sums_ref[...] = jnp.zeros_like(sums_ref)

    for c in range(rays // block):
        at = pl.ds(c * span, span)
        ray_at = pl.ds(c * block, block)
        rank = rel_ref[:, ray_at]
        decays = gathered_ref[:, 0, ray_at]
        products = gathered_ref[:, 1, ray_at]
        ahead = jnp.zeros((parts, block), F32)
        for q in range(parts):
            ahead = ahead + jnp.where(rank[q : q + 1] < rank, decays[q : q + 1], 0.0)
        prefixes = jnp.exp(ahead)
        share = prefixes * products
        tail = jnp.sum(jnp.where(rank > rank[0:1], share, 0.0), axis=0, keepdims=True)
        prefix = prefixes[0:1]

        logit = logit_ref[:, ray_at]
        grown = jnp.exp(-jnp.abs(logit))
        density = jnp.maximum(logit, 0.0) + jnp.log1p(grown)
        slope = jnp.where(logit >= 0, 1.0, grown) / (1.0 + grown)
        place = lax.broadcasted_iota(jnp.int32, (slots, block), 0)
        live = place < counts_ref[:, ray_at]
        optical = jnp.where(live, density * step_length, 0.0)
        reach = jnp.exp(-before_of(optical))
        passed = jnp.exp(-optical)
        blend = reach * (1.0 - passed)
        grad_blend = prefix * side_ref[:, ray_at]
        lost = blend * grad_blend
        after = jnp.zeros_like(lost)
        for j in range(1, slots):
            after = after + jnp.where(place < j, lost[j : j + 1], 0.0)
        grad_optical = reach * passed * grad_blend - after - tail
        grad_logit = jnp.where(live, grad_optical * step_length, 0.0) * slope
        cols = columns(jnp.concatenate([blend * prefix, grad_logit, prefix, jnp.zeros((7, block), F32)], axis=0), block)
        cot = cot_ref[ray_at, :]
        shaded = cols[2 * slots] * colour_ref[ray_at, :]
        for n in range(block // per):
            owner = c * (block // per) + n
            shaded_ref[pl.ds((owner ^ space) & 1, 1), pl.ds(owner >> 1, 1)] = shaded[n * per : (n + 1) * per][None, None]
        below = hidden_ref[top, at, :]
        grads = []
        head_sum = jnp.zeros((block, width), F32)
        bias_sum = jnp.zeros((block, width), F32)
        for i in range(slots):
            grad = cols[i] * cot + cols[slots + i] * head
            bias_sum = bias_sum + grad
            head_sum = head_sum + cols[slots + i] * below[i * block : (i + 1) * block].astype(F32)
            grads.append(grad.astype(BF16))
        logit_sum = jnp.sum(jnp.sum(grad_logit, axis=0, keepdims=True), axis=1, keepdims=True)
        sums_ref[0:1, :] += jnp.sum(bias_sum, axis=0, keepdims=True)
        sums_ref[1:2, :] += jnp.sum(head_sum, axis=0, keepdims=True)
        sums_ref[3:4, :] += jnp.broadcast_to(logit_sum, (1, width))
        half = jnp.concatenate(grads, axis=0)
        acc_top[...] += mat_grad(below, half)
        grad = layer_back(half, below, mats_ref, top)
        sums_ref[2:3, :] += jnp.sum(grad, axis=0, keepdims=True)
        half = grad.astype(BF16)
        half_ref[at, :] = half
        acc_next[...] += mat_grad(hidden_ref[top - 1, at, :], half)

    me = lax.axis_index("ray")
    store_pieces(pieces_ref, 0, acc_top[...], me)
    store_pieces(pieces_ref, 1, acc_next[...], me)
    mixed = jnp.dot(
        sums_ref[...], mats_ref[top].astype(F32), precision=lax.Precision.HIGHEST, preferred_element_type=F32
    )
    sums_ref[1:2, :] = mixed[1:2, :] + sums_ref[3:4, :] * bias_ref[top : top + 1, :]


def low_kernel(half_ref, sums_ref, mats_ref, hidden_ref, pieces_ref, acc_a, acc_b, bias_ref):
    rows = half_ref.shape[0]
    span = LOW_SPAN
    acc_a[...] = jnp.zeros_like(acc_a)
    acc_b[...] = jnp.zeros_like(acc_b)
    bias_ref[...] = jnp.zeros_like(bias_ref)

    for c in range(rows // span):
        at = pl.ds(c * span, span)
        grad = layer_back(half_ref[at, :], hidden_ref[2, at, :], mats_ref, 2)
        bias_ref[0:1, :] += jnp.sum(grad, axis=0, keepdims=True)
        half = grad.astype(BF16)
        below = hidden_ref[1, at, :]
        acc_a[...] += mat_grad(below, half)
        grad = layer_back(half, below, mats_ref, 1)
        bias_ref[1:2, :] += jnp.sum(grad, axis=0, keepdims=True)
        half = grad.astype(BF16)
        acc_b[...] += mat_grad(hidden_ref[0, at, :], half)

    me = lax.axis_index("ray")
    store_pieces(pieces_ref, 0, acc_a[...], me)
    store_pieces(pieces_ref, 1, acc_b[...], me)
    count = pieces_ref.shape[0]
    first = 2 * (acc_a.shape[0] // count)
    small = jnp.concatenate(
        [sums_ref[0:3, :], bias_ref[0:2, :], jnp.zeros((3, acc_a.shape[1]), F32)], axis=0
    )
    for k in range(count):
        pieces_ref[k, first : first + 8, :] = small


def fold_kernel(step, kept_ref, other_ref, out_ref):
    bit = (lax.axis_index("space") // step) & 1
    for j in range(other_ref.shape[0]):
        out_ref[pl.ds((j & 1) ^ bit, 1), j >> 1] = (kept_ref[0, j] + other_ref[j])[None]


def join_kernel(*refs):
    *inputs, small_ref, kept_ref, other_ref, out_ref, bias_ref, head_ref, composite_ref = refs
    me = lax.axis_index("ray")
    layers, width = out_ref.shape[:2]
    count = len(inputs) // 2
    rows = width // count
    for chunk in range(2):
        for k in range(count):
            piece = inputs[chunk * count + k]
            at = pl.ds(pl.multiple_of((me ^ k) * rows, rows), rows)
            for slot in range(2):
                out_ref[layers - 1 - 2 * chunk - slot, at, :] = piece[slot * rows : (slot + 1) * rows, :]
    first = 2 * rows
    bias_ref[...] = jnp.concatenate(
        [small_ref[first + n : first + n + 1, :] for n in (4, 3, 2, 0)], axis=0
    )
    head_ref[...] = small_ref[first + 1 : first + 2, :]
    composite_ref[...] = kept_ref[0, 0] + other_ref[0]


def partners(count, k):
    return [(i, i ^ k) for i in range(count)]


def on_device(
    grid_table, weights, biases, density_head, sample_cells, sample_counts, ray_order, cotangent
):
    table = grid_table[0]
    mats = weights[0]
    bias = biases[0]
    slots = sample_cells.shape[2]
    cells = sample_cells[0].T.reshape(slots, -1, RAY_BLOCK).transpose(1, 0, 2).reshape(-1, RAY_BLOCK)
    counts = sample_counts.T
    order = ray_order.T
    parts = lax.axis_size("space")
    ray_parts = lax.axis_size("ray")
    layers, width = bias.shape
    rays = sample_cells.shape[1]
    rows = slots * rays
    span = slots * RAY_BLOCK
    shape = jax.ShapeDtypeStruct
    grant = pltpu.CompilerParams(vmem_limit_bytes=GRANT)

    inputs = (cells, counts, order, table, mats, bias, density_head, cotangent)
    hidden, logit, side, pack, rel, colour, counts, mats, bias, head, cot = pl.pallas_call(
        forward_kernel,
        out_shape=(
            shape((layers, rows, width), BF16),
            shape((slots, rays), F32),
            shape((slots, rays), F32),
            shape((2, rays), F32),
            shape((parts, rays), jnp.int32),
            shape((rays, width), F32),
            shape(counts.shape, jnp.int32),
            shape(mats.shape, BF16),
            shape(bias.shape, F32),
            shape(density_head.shape, F32),
            shape(cotangent.shape, F32),
        ),
        in_specs=[HBM] * 8,
        out_specs=(VMEM,) * 11,
        scratch_shapes=[
            pltpu.SMEM(cells.shape, jnp.int32),
            pltpu.VMEM(cells.shape, jnp.int32),
            pltpu.VMEM((parts, rays), jnp.int32),
            pltpu.VMEM(table.shape, BF16),
            pltpu.VMEM((2 * table.shape[0], width // 2), F32),
            pltpu.VMEM((2 * span, width // 2), F32),
            pltpu.SemaphoreType.DMA((6,)),
            pltpu.SemaphoreType.DMA((4,)),
            pltpu.SemaphoreType.DMA((2,)),
        ],
        compiler_params=grant,
        name="forward",
    )(*[pltpu.with_memory_space_constraint(x, pltpu.HBM) for x in inputs])

    gathered = pack[None]
    step = 1
    while step < parts:
        other = lax.ppermute(gathered, "space", partners(parts, step))
        gathered = jnp.concatenate([gathered, other], axis=0)
        step *= 2

    piece_rows = width // ray_parts
    top_pieces, half, sums, shaded = pl.pallas_call(
        top_kernel,
        out_shape=(
            shape((ray_parts, 2 * piece_rows, width), F32),
            shape((rows, width), BF16),
            shape((8, width), F32),
            shape((2, parts // 2, rays // parts, width), F32),
        ),
        in_specs=[VMEM] * 11,
        out_specs=(VMEM,) * 4,
        scratch_shapes=[pltpu.VMEM((width, width), F32)] * 2,
        compiler_params=grant,
        name="top",
    )(gathered, rel, counts, logit, side, cot, colour, head, bias, mats, hidden)

    def shift(array, axis, count, k):
        return lax.ppermute(array, axis, partners(count, k))

    top_got = [shift(top_pieces[k], "ray", ray_parts, k) for k in range(1, ray_parts)]

    low_pieces = pl.pallas_call(
        low_kernel,
        out_shape=shape((ray_parts, 2 * piece_rows + 8, width), F32),
        in_specs=[VMEM] * 4,
        out_specs=VMEM,
        scratch_shapes=[pltpu.VMEM((width, width), F32)] * 2 + [pltpu.VMEM((8, width), F32)],
        compiler_params=grant,
        name="low",
    )(half, sums, mats, hidden)

    low_got = [shift(low_pieces[k], "ray", ray_parts, k) for k in range(1, ray_parts)]

    top_own = top_pieces[0] + sum(top_got[1:], top_got[0])
    low_own = low_pieces[0] + sum(low_got[1:], low_got[0])
    small = low_own
    low_own = low_own[: 2 * piece_rows]
    top_all = [top_own] + [shift(top_own, "ray", ray_parts, k) for k in range(1, ray_parts)]
    low_all = [low_own] + [shift(low_own, "ray", ray_parts, k) for k in range(1, ray_parts)]

    step = 1
    other = shift(shaded[1], "space", parts, step)
    while 2 * step < parts:
        step *= 2
        count, per = other.shape[0], other.shape[1]
        shaded = pl.pallas_call(
            functools.partial(fold_kernel, step),
            out_shape=shape((2, count // 2, per, width), F32),
            in_specs=[VMEM] * 2,
            out_specs=VMEM,
            compiler_params=pltpu.CompilerParams(vmem_limit_bytes=4 << 20),
            name="fold",
        )(shaded, other)
        other = shift(shaded[1], "space", parts, step)

    weight_grads, bias_grads, head_grads, composite = pl.pallas_call(
        join_kernel,
        out_shape=(
            shape((layers, width, width), F32),
            shape((layers, width), F32),
            shape((1, width), F32),
            shape((rays // parts, width), F32),
        ),
        in_specs=[VMEM] * (2 * ray_parts + 3),
        out_specs=(VMEM,) * 4,
        compiler_params=pltpu.CompilerParams(vmem_limit_bytes=8 << 20),
        name="join",
    )(*top_all, *low_all, small, shaded, other)

    return (composite, weight_grads[None], bias_grads[None], head_grads)


def solution(mesh):
    placed = (
        P("space", None, None),
        P("space", None, None, None),
        P("space", None, None),
        P("space", None),
        P("space", "ray", None),
        P("ray", "space"),
        P("ray", None),
        P("ray", None),
    )
    return jax.shard_map(
        on_device,
        mesh=mesh,
        in_specs=placed,
        out_specs=(
            P(("ray", "space"), None),
            P("space", None, None, None),
            P("space", None, None),
            P("space", None),
        ),
        check_vma=False,
    )
```

```python
import functools

import jax
import jax.numpy as jnp
from jax import lax
from jax.experimental import pallas as pl
from jax.experimental.pallas import tpu as pltpu
from jax.sharding import PartitionSpec as P

step_length = 0.05
RAY_BLOCK = 128
GATHER_UNROLL = 64
LOW_SPAN = 1024
GRANT = 20 << 20

F32 = jnp.float32
BF16 = jnp.bfloat16
VMEM = pl.BlockSpec(memory_space=pltpu.VMEM)
SMEM = pl.BlockSpec(memory_space=pltpu.SMEM)
HBM = pl.BlockSpec(memory_space=pltpu.HBM)


def columns(rows, block):
    n = rows.shape[0]
    square = jnp.concatenate([rows, jnp.zeros((block - n, block), F32)], axis=0).T
    return [square[:, i : i + 1] for i in range(n)]


def row_block(cols, block):
    lane = lax.broadcasted_iota(jnp.int32, (block, block), 1)
    square = jnp.zeros((block, block), F32)
    for i, col in enumerate(cols):
        square = jnp.where(lane == i, col, square)
    return square.T[: len(cols)]


def before_of(optical):
    slots = optical.shape[0]
    place = lax.broadcasted_iota(jnp.int32, optical.shape, 0)
    total = jnp.zeros_like(optical)
    for j in range(slots - 1):
        total = total + jnp.where(place > j, optical[j : j + 1], 0.0)
    return total


def forward_kernel(
    cells_hbm, counts_hbm, order_hbm, table_hbm, mats_hbm, bias_hbm, head_hbm, cot_hbm,
    hidden_ref, logit_ref, side_ref, pack_ref, rel_ref, colour_ref, counts_ref, mats_ref, bias_ref, head_ref, cot_ref,
    cells_ref, cells_vmem, order_ref, table_ref, wide_table, rows_ref, small_sem, table_sem, cell_sem,
):
    layers, width = bias_ref.shape
    parts, rays = order_ref.shape
    block = RAY_BLOCK
    span = rows_ref.shape[0] // 2
    slots = span // block
    half = width // 2
    cells = table_ref.shape[0]
    pieces = table_sem.shape[0]
    piece = cells // pieces
    cells_per = 256

    fetch = pltpu.make_async_copy(cells_hbm, cells_vmem, cell_sem.at[0])
    fetch.start()
    table_copies = []
    for t in range(pieces):
        at = pl.ds(t * piece, piece)
        table_copies.append(pltpu.make_async_copy(table_hbm.at[at], table_ref.at[at], table_sem.at[t]))
        table_copies[-1].start()
    copies = []
    pairs = (
        (order_hbm, order_ref), (mats_hbm, mats_ref), (bias_hbm, bias_ref), (head_hbm, head_ref), (cot_hbm, cot_ref),
        (counts_hbm, counts_ref),
    )
    for t, (source, target) in enumerate(pairs):
        copies.append(pltpu.make_async_copy(source, target, small_sem.at[t]))
        copies[-1].start()

    fetch.wait()
    cells_vmem[...] = cells_vmem[...] * 2
    settle = pltpu.make_async_copy(cells_vmem, cells_ref, cell_sem.at[1])
    settle.start()
    for t in range(pieces):
        table_copies[t].wait()

        @pl.loop(0, piece // cells_per)
        def _(n):
            at = pl.multiple_of(t * piece + n * cells_per, cells_per)
            wide = table_ref[pl.ds(at, cells_per), :].astype(F32)
            for side in range(2):
                wide_table[pl.ds(2 * at + side, cells_per, stride=2), :] = wide[:, side * half : (side + 1) * half]

    settle.wait()

    def gather(first, count):
        for u in range(count):
            at = first + u
            rows_ref[2 * u : 2 * u + 2, :] = wide_table[pl.ds(cells_ref[at // block, at % block], 2), :]

    gather(0, span)
    for copy in copies:
        copy.wait()
    me = lax.axis_index("space")
    for k in range(parts):
        rel_ref[k : k + 1, :] = order_ref[pl.ds(me ^ k, 1), :]

    def compute(c, more):
        at = pl.ds(c * span, span)
        ray_at = pl.ds(c * block, block)
        head = head_ref[...]
        hidden = jnp.concatenate(
            [rows_ref[pl.ds(side, span, stride=2), :].astype(BF16) for side in range(2)], axis=1
        )
        if more:
            gather((c + 1) * span, span)
        linear = None
        for layer in range(layers):
            hidden_ref[layer, at, :] = hidden
            linear = jnp.dot(hidden, mats_ref[layer], preferred_element_type=F32) + bias_ref[layer : layer + 1, :]
            if layer + 1 < layers:
                hidden = jnp.maximum(linear, 0.0).astype(BF16)
        cot = cot_ref[ray_at, :]
        cols = []
        for i in range(slots):
            cols.append(jnp.sum(linear[i * block : (i + 1) * block] * head, axis=1, keepdims=True))
        for i in range(slots):
            cols.append(jnp.sum(linear[i * block : (i + 1) * block] * cot, axis=1, keepdims=True))
        both = row_block(cols, block)
        logit = both[:slots]
        side = both[slots:]
        density = jnp.maximum(logit, 0.0) + jnp.log1p(jnp.exp(-jnp.abs(logit)))
        place = lax.broadcasted_iota(jnp.int32, (slots, block), 0)
        live = place < counts_ref[:, ray_at]
        optical = jnp.where(live, density * step_length, 0.0)
        blend = jnp.exp(-before_of(optical)) * (1.0 - jnp.exp(-optical))
        logit_ref[:, ray_at] = logit
        side_ref[:, ray_at] = side
        pack_ref[0:1, ray_at] = -jnp.sum(optical, axis=0, keepdims=True)
        pack_ref[1:2, ray_at] = jnp.sum(blend * side, axis=0, keepdims=True)
        colour = jnp.zeros((block, width), F32)
        for i, col in enumerate(columns(blend, block)):
            colour = colour + col * linear[i * block : (i + 1) * block]
        colour_ref[ray_at, :] = colour

    steps = rays // block

    for c in range(steps):
        compute(c, c + 1 < steps)


def layer_back(half, below, mats, layer):
    back = lax.dot_general(half, mats[layer], (((1,), (1,)), ((), ())), preferred_element_type=F32)
    return jnp.where(below > 0, back.astype(BF16), jnp.zeros((), BF16))


def row_sum(half):
    return jnp.dot(jnp.ones((8, half.shape[0]), BF16), half, preferred_element_type=F32)[0:1]


def mat_grad(below, half):
    return lax.dot_general(below, half, (((0,), (0,)), ((), ())), preferred_element_type=F32)


def store_pieces(pieces_ref, slot, total, me):
    count = pieces_ref.shape[0]
    rows = total.shape[0] // count
    for owner in range(count):
        pieces_ref[pl.ds(owner ^ me, 1), slot * rows : (slot + 1) * rows, :] = total[owner * rows : (owner + 1) * rows][None]


def top_kernel(
    gathered_ref, rel_ref, counts_ref, logit_ref, side_ref, cot_ref, colour_ref, head_ref, bias_ref, mats_ref, hidden_ref,
    pieces_ref, half_ref, sums_ref, shaded_ref,
    acc_top, acc_next,
):
    layers = mats_ref.shape[0]
    top = layers - 1
    slots, rays = logit_ref.shape
    parts = rel_ref.shape[0]
    width = head_ref.shape[1]
    block = RAY_BLOCK
    span = slots * block
    head = head_ref[...]
    space = lax.axis_index("space")
    per = rays // parts
    acc_top[...] = jnp.zeros_like(acc_top)
    acc_next[...] = jnp.zeros_like(acc_next)
    sums_ref[...] = jnp.zeros_like(sums_ref)

    for c in range(rays // block):
        at = pl.ds(c * span, span)
        ray_at = pl.ds(c * block, block)
        rank = rel_ref[:, ray_at]
        decays = gathered_ref[:, 0, ray_at]
        products = gathered_ref[:, 1, ray_at]
        ahead = jnp.zeros((parts, block), F32)
        for q in range(parts):
            ahead = ahead + jnp.where(rank[q : q + 1] < rank, decays[q : q + 1], 0.0)
        prefixes = jnp.exp(ahead)
        share = prefixes * products
        tail = jnp.sum(jnp.where(rank > rank[0:1], share, 0.0), axis=0, keepdims=True)
        prefix = prefixes[0:1]

        logit = logit_ref[:, ray_at]
        grown = jnp.exp(-jnp.abs(logit))
        density = jnp.maximum(logit, 0.0) + jnp.log1p(grown)
        slope = jnp.where(logit >= 0, 1.0, grown) / (1.0 + grown)
        place = lax.broadcasted_iota(jnp.int32, (slots, block), 0)
        live = place < counts_ref[:, ray_at]
        optical = jnp.where(live, density * step_length, 0.0)
        reach = jnp.exp(-before_of(optical))
        passed = jnp.exp(-optical)
        blend = reach * (1.0 - passed)
        grad_blend = prefix * side_ref[:, ray_at]
        lost = blend * grad_blend
        after = jnp.zeros_like(lost)
        for j in range(1, slots):
            after = after + jnp.where(place < j, lost[j : j + 1], 0.0)
        grad_optical = reach * passed * grad_blend - after - tail
        grad_logit = jnp.where(live, grad_optical * step_length, 0.0) * slope
        weight = blend * prefix
        weight_sum = jnp.sum(weight, axis=0, keepdims=True)
        cols = columns(
            jnp.concatenate([weight, grad_logit, prefix, weight_sum, jnp.zeros((6, block), F32)], axis=0), block
        )
        cot = cot_ref[ray_at, :]
        shaded = cols[2 * slots] * colour_ref[ray_at, :]
        for n in range(block // per):
            owner = c * (block // per) + n
            shaded_ref[pl.ds((owner ^ space) & 1, 1), pl.ds(owner >> 1, 1)] = shaded[n * per : (n + 1) * per][None, None]
        below = hidden_ref[top, at, :]
        grads = []
        for i in range(slots):
            grads.append((cols[i] * cot + cols[slots + i] * head).astype(BF16))
        logit_sum = jnp.sum(jnp.sum(grad_logit, axis=0, keepdims=True), axis=1, keepdims=True)
        line = jnp.concatenate([grad_logit[i : i + 1] for i in range(slots)], axis=1)
        lines = []
        for _ in range(3):
            lines.append(line.astype(BF16).astype(F32))
            line = line - lines[-1]
        lines = jnp.concatenate(lines + [jnp.zeros((5, span), F32)], axis=0).astype(BF16)
        head_sum = jnp.sum(jnp.dot(lines, below, preferred_element_type=F32), axis=0, keepdims=True)
        bias_sum = jnp.sum(cols[2 * slots + 1] * cot, axis=0, keepdims=True)
        sums_ref[0:1, :] += bias_sum + logit_sum * head
        sums_ref[1:2, :] += head_sum
        sums_ref[3:4, :] += jnp.broadcast_to(logit_sum, (1, width))
        half = jnp.concatenate(grads, axis=0)
        acc_top[...] += mat_grad(below, half)
        half = layer_back(half, below, mats_ref, top)
        sums_ref[2:3, :] += row_sum(half)
        half_ref[at, :] = half
        acc_next[...] += mat_grad(hidden_ref[top - 1, at, :], half)

    me = lax.axis_index("ray")
    store_pieces(pieces_ref, 0, acc_top[...], me)
    store_pieces(pieces_ref, 1, acc_next[...], me)
    mixed = jnp.dot(
        sums_ref[...], mats_ref[top].astype(F32), precision=lax.Precision.HIGHEST, preferred_element_type=F32
    )
    sums_ref[1:2, :] = mixed[1:2, :] + sums_ref[3:4, :] * bias_ref[top : top + 1, :]


def low_kernel(half_ref, sums_ref, mats_ref, hidden_ref, pieces_ref, acc_a, acc_b, bias_ref):
    rows = half_ref.shape[0]
    span = LOW_SPAN
    acc_a[...] = jnp.zeros_like(acc_a)
    acc_b[...] = jnp.zeros_like(acc_b)
    bias_ref[...] = jnp.zeros_like(bias_ref)

    for c in range(rows // span):
        at = pl.ds(c * span, span)
        half = layer_back(half_ref[at, :], hidden_ref[2, at, :], mats_ref, 2)
        bias_ref[0:1, :] += row_sum(half)
        below = hidden_ref[1, at, :]
        acc_a[...] += mat_grad(below, half)
        half = layer_back(half, below, mats_ref, 1)
        bias_ref[1:2, :] += row_sum(half)
        acc_b[...] += mat_grad(hidden_ref[0, at, :], half)

    me = lax.axis_index("ray")
    store_pieces(pieces_ref, 0, acc_a[...], me)
    store_pieces(pieces_ref, 1, acc_b[...], me)
    count = pieces_ref.shape[0]
    first = 2 * (acc_a.shape[0] // count)
    small = jnp.concatenate(
        [sums_ref[0:3, :], bias_ref[0:2, :], jnp.zeros((3, acc_a.shape[1]), F32)], axis=0
    )
    for k in range(count):
        pieces_ref[k, first : first + 8, :] = small


def fold_kernel(step, kept_ref, other_ref, out_ref):
    bit = (lax.axis_index("space") // step) & 1
    for j in range(other_ref.shape[0]):
        out_ref[pl.ds((j & 1) ^ bit, 1), j >> 1] = (kept_ref[0, j] + other_ref[j])[None]


def join_kernel(*refs):
    *inputs, small_ref, kept_ref, other_ref, out_ref, bias_ref, head_ref, composite_ref = refs
    me = lax.axis_index("ray")
    layers, width = out_ref.shape[:2]
    count = len(inputs) // 2
    rows = width // count
    for chunk in range(2):
        for k in range(count):
            piece = inputs[chunk * count + k]
            at = pl.ds(pl.multiple_of((me ^ k) * rows, rows), rows)
            for slot in range(2):
                out_ref[layers - 1 - 2 * chunk - slot, at, :] = piece[slot * rows : (slot + 1) * rows, :]
    first = 2 * rows
    bias_ref[...] = jnp.concatenate(
        [small_ref[first + n : first + n + 1, :] for n in (4, 3, 2, 0)], axis=0
    )
    head_ref[...] = small_ref[first + 1 : first + 2, :]
    composite_ref[...] = kept_ref[0, 0] + other_ref[0]


def partners(count, k):
    return [(i, i ^ k) for i in range(count)]


def on_device(
    grid_table, weights, biases, density_head, sample_cells, sample_counts, ray_order, cotangent
):
    table = grid_table[0]
    mats = weights[0]
    bias = biases[0]
    slots = sample_cells.shape[2]
    cells = sample_cells[0].T.reshape(slots, -1, RAY_BLOCK).transpose(1, 0, 2).reshape(-1, RAY_BLOCK)
    counts = sample_counts.T
    order = ray_order.T
    parts = lax.axis_size("space")
    ray_parts = lax.axis_size("ray")
    layers, width = bias.shape
    rays = sample_cells.shape[1]
    rows = slots * rays
    span = slots * RAY_BLOCK
    shape = jax.ShapeDtypeStruct
    grant = pltpu.CompilerParams(vmem_limit_bytes=GRANT)

    inputs = (cells, counts, order, table, mats, bias, density_head, cotangent)
    hidden, logit, side, pack, rel, colour, counts, mats, bias, head, cot = pl.pallas_call(
        forward_kernel,
        out_shape=(
            shape((layers, rows, width), BF16),
            shape((slots, rays), F32),
            shape((slots, rays), F32),
            shape((2, rays), F32),
            shape((parts, rays), jnp.int32),
            shape((rays, width), F32),
            shape(counts.shape, jnp.int32),
            shape(mats.shape, BF16),
            shape(bias.shape, F32),
            shape(density_head.shape, F32),
            shape(cotangent.shape, F32),
        ),
        in_specs=[HBM] * 8,
        out_specs=(VMEM,) * 11,
        scratch_shapes=[
            pltpu.SMEM(cells.shape, jnp.int32),
            pltpu.VMEM(cells.shape, jnp.int32),
            pltpu.VMEM((parts, rays), jnp.int32),
            pltpu.VMEM(table.shape, BF16),
            pltpu.VMEM((2 * table.shape[0], width // 2), F32),
            pltpu.VMEM((2 * span, width // 2), F32),
            pltpu.SemaphoreType.DMA((6,)),
            pltpu.SemaphoreType.DMA((4,)),
            pltpu.SemaphoreType.DMA((2,)),
        ],
        compiler_params=grant,
        name="forward",
    )(*[pltpu.with_memory_space_constraint(x, pltpu.HBM) for x in inputs])

    gathered = pack[None]
    step = 1
    while step < parts:
        other = lax.ppermute(gathered, "space", partners(parts, step))
        gathered = jnp.concatenate([gathered, other], axis=0)
        step *= 2

    piece_rows = width // ray_parts
    top_pieces, half, sums, shaded = pl.pallas_call(
        top_kernel,
        out_shape=(
            shape((ray_parts, 2 * piece_rows, width), F32),
            shape((rows, width), BF16),
            shape((8, width), F32),
            shape((2, parts // 2, rays // parts, width), F32),
        ),
        in_specs=[VMEM] * 11,
        out_specs=(VMEM,) * 4,
        scratch_shapes=[pltpu.VMEM((width, width), F32)] * 2,
        compiler_params=grant,
        name="top",
    )(gathered, rel, counts, logit, side, cot, colour, head, bias, mats, hidden)

    def shift(array, axis, count, k):
        return lax.ppermute(array, axis, partners(count, k))

    top_got = [shift(top_pieces[k], "ray", ray_parts, k) for k in range(1, ray_parts)]

    low_pieces = pl.pallas_call(
        low_kernel,
        out_shape=shape((ray_parts, 2 * piece_rows + 8, width), F32),
        in_specs=[VMEM] * 4,
        out_specs=VMEM,
        scratch_shapes=[pltpu.VMEM((width, width), F32)] * 2 + [pltpu.VMEM((8, width), F32)],
        compiler_params=grant,
        name="low",
    )(half, sums, mats, hidden)

    low_got = [shift(low_pieces[k], "ray", ray_parts, k) for k in range(1, ray_parts)]

    top_own = top_pieces[0] + sum(top_got[1:], top_got[0])
    low_own = low_pieces[0] + sum(low_got[1:], low_got[0])
    small = low_own
    low_own = low_own[: 2 * piece_rows]
    top_all = [top_own] + [shift(top_own, "ray", ray_parts, k) for k in range(1, ray_parts)]
    low_all = [low_own] + [shift(low_own, "ray", ray_parts, k) for k in range(1, ray_parts)]

    step = 1
    other = shift(shaded[1], "space", parts, step)
    while 2 * step < parts:
        step *= 2
        count, per = other.shape[0], other.shape[1]
        shaded = pl.pallas_call(
            functools.partial(fold_kernel, step),
            out_shape=shape((2, count // 2, per, width), F32),
            in_specs=[VMEM] * 2,
            out_specs=VMEM,
            compiler_params=pltpu.CompilerParams(vmem_limit_bytes=4 << 20),
            name="fold",
        )(shaded, other)
        other = shift(shaded[1], "space", parts, step)

    weight_grads, bias_grads, head_grads, composite = pl.pallas_call(
        join_kernel,
        out_shape=(
            shape((layers, width, width), F32),
            shape((layers, width), F32),
            shape((1, width), F32),
            shape((rays // parts, width), F32),
        ),
        in_specs=[VMEM] * (2 * ray_parts + 3),
        out_specs=(VMEM,) * 4,
        compiler_params=pltpu.CompilerParams(vmem_limit_bytes=8 << 20),
        name="join",
    )(*top_all, *low_all, small, shaded, other)

    return (composite, weight_grads[None], bias_grads[None], head_grads)


def solution(mesh):
    placed = (
        P("space", None, None),
        P("space", None, None, None),
        P("space", None, None),
        P("space", None),
        P("space", "ray", None),
        P("ray", "space"),
        P("ray", None),
        P("ray", None),
    )
    return jax.shard_map(
        on_device,
        mesh=mesh,
        in_specs=placed,
        out_specs=(
            P(("ray", "space"), None),
            P("space", None, None, None),
            P("space", None, None),
            P("space", None),
        ),
        check_vma=False,
    )
```

```python
import functools

import jax
import jax.numpy as jnp
from jax import lax
from jax.experimental import pallas as pl
from jax.experimental.pallas import tpu as pltpu
from jax.sharding import PartitionSpec as P

step_length = 0.05
RAY_BLOCK = 128
GATHER_UNROLL = 64
LOW_SPAN = 1024
GRANT = 20 << 20

F32 = jnp.float32
BF16 = jnp.bfloat16
VMEM = pl.BlockSpec(memory_space=pltpu.VMEM)
SMEM = pl.BlockSpec(memory_space=pltpu.SMEM)
HBM = pl.BlockSpec(memory_space=pltpu.HBM)


def columns(rows, block):
    n = rows.shape[0]
    square = jnp.concatenate([rows, jnp.zeros((block - n, block), F32)], axis=0).T
    return [square[:, i : i + 1] for i in range(n)]


def three_parts(row):
    parts = []
    for _ in range(3):
        parts.append(row.astype(BF16).astype(F32))
        row = row - parts[-1]
    return jnp.concatenate(parts + [jnp.zeros((5, row.shape[1]), F32)], axis=0).astype(BF16)


def row_block(cols, block):
    lane = lax.broadcasted_iota(jnp.int32, (block, block), 1)
    square = jnp.zeros((block, block), F32)
    for i, col in enumerate(cols):
        square = jnp.where(lane == i, col, square)
    return square.T[: len(cols)]


def before_of(optical):
    slots = optical.shape[0]
    place = lax.broadcasted_iota(jnp.int32, optical.shape, 0)
    total = jnp.zeros_like(optical)
    for j in range(slots - 1):
        total = total + jnp.where(place > j, optical[j : j + 1], 0.0)
    return total


def forward_kernel(
    cells_hbm, counts_hbm, order_hbm, table_hbm, mats_hbm, bias_hbm, head_hbm, cot_hbm,
    hidden_ref, logit_ref, side_ref, pack_ref, rel_ref, colour_ref, counts_ref, mats_ref, bias_ref, head_ref, cot_ref,
    cells_ref, cells_vmem, order_ref, table_ref, wide_table, rows_ref, small_sem, table_sem, cell_sem,
):
    layers, width = bias_ref.shape
    parts, rays = order_ref.shape
    block = RAY_BLOCK
    span = rows_ref.shape[0] // 2
    slots = span // block
    half = width // 2
    cells = table_ref.shape[0]
    pieces = table_sem.shape[0]
    piece = cells // pieces
    cells_per = 256

    fetch = pltpu.make_async_copy(cells_hbm, cells_vmem, cell_sem.at[0])
    fetch.start()
    table_copies = []
    for t in range(pieces):
        at = pl.ds(t * piece, piece)
        table_copies.append(pltpu.make_async_copy(table_hbm.at[at], table_ref.at[at], table_sem.at[t]))
        table_copies[-1].start()
    copies = []
    pairs = (
        (order_hbm, order_ref), (mats_hbm, mats_ref), (bias_hbm, bias_ref), (head_hbm, head_ref), (cot_hbm, cot_ref),
        (counts_hbm, counts_ref),
    )
    for t, (source, target) in enumerate(pairs):
        copies.append(pltpu.make_async_copy(source, target, small_sem.at[t]))
        copies[-1].start()

    fetch.wait()
    cells_vmem[...] = cells_vmem[...] * 2
    settle = pltpu.make_async_copy(cells_vmem, cells_ref, cell_sem.at[1])
    settle.start()
    for t in range(pieces):
        table_copies[t].wait()

        @pl.loop(0, piece // cells_per)
        def _(n):
            at = pl.multiple_of(t * piece + n * cells_per, cells_per)
            wide = table_ref[pl.ds(at, cells_per), :].astype(F32)
            for side in range(2):
                wide_table[pl.ds(2 * at + side, cells_per, stride=2), :] = wide[:, side * half : (side + 1) * half]

    settle.wait()

    def gather(first, count):
        for u in range(count):
            at = first + u
            rows_ref[2 * u : 2 * u + 2, :] = wide_table[pl.ds(cells_ref[at // block, at % block], 2), :]

    gather(0, span)
    for copy in copies:
        copy.wait()
    me = lax.axis_index("space")
    for k in range(parts):
        rel_ref[k : k + 1, :] = order_ref[pl.ds(me ^ k, 1), :]

    head = head_ref[...]
    across = (((1,), (1,)), ((), ()))
    seen = lax.dot_general(three_parts(head), mats_ref[layers - 1], across, preferred_element_type=F32)
    seen = three_parts(jnp.sum(seen, axis=0, keepdims=True))
    offset = jnp.sum(head * bias_ref[layers - 1 : layers, :], axis=1, keepdims=True)

    def compute(c, more):
        at = pl.ds(c * span, span)
        ray_at = pl.ds(c * block, block)
        hidden = jnp.concatenate(
            [rows_ref[pl.ds(side, span, stride=2), :].astype(BF16) for side in range(2)], axis=1
        )
        if more:
            gather((c + 1) * span, span)
        linear = None
        for layer in range(layers):
            hidden_ref[layer, at, :] = hidden
            linear = jnp.dot(hidden, mats_ref[layer], preferred_element_type=F32) + bias_ref[layer : layer + 1, :]
            if layer + 1 < layers:
                hidden = jnp.maximum(linear, 0.0).astype(BF16)
        cot = cot_ref[ray_at, :]
        line = lax.dot_general(seen, hidden, across, preferred_element_type=F32)
        line = jnp.sum(line, axis=0, keepdims=True) + offset
        logit = jnp.concatenate([line[:, i * block : (i + 1) * block] for i in range(slots)], axis=0)
        cols = []
        for i in range(slots):
            cols.append(jnp.sum(linear[i * block : (i + 1) * block] * cot, axis=1, keepdims=True))
        side = row_block(cols, block)
        density = jnp.maximum(logit, 0.0) + jnp.log1p(jnp.exp(-jnp.abs(logit)))
        place = lax.broadcasted_iota(jnp.int32, (slots, block), 0)
        live = place < counts_ref[:, ray_at]
        optical = jnp.where(live, density * step_length, 0.0)
        blend = jnp.exp(-before_of(optical)) * (1.0 - jnp.exp(-optical))
        logit_ref[:, ray_at] = logit
        side_ref[:, ray_at] = side
        pack_ref[0:1, ray_at] = -jnp.sum(optical, axis=0, keepdims=True)
        pack_ref[1:2, ray_at] = jnp.sum(blend * side, axis=0, keepdims=True)
        colour = jnp.zeros((block, width), F32)
        for i, col in enumerate(columns(blend, block)):
            colour = colour + col * linear[i * block : (i + 1) * block]
        colour_ref[ray_at, :] = colour

    steps = rays // block

    for c in range(steps):
        compute(c, c + 1 < steps)


def layer_back(half, below, mats, layer):
    back = lax.dot_general(half, mats[layer], (((1,), (1,)), ((), ())), preferred_element_type=F32)
    return jnp.where(below > 0, back.astype(BF16), jnp.zeros((), BF16))


def row_sum(half):
    return jnp.dot(jnp.ones((8, half.shape[0]), BF16), half, preferred_element_type=F32)[0:1]


def mat_grad(below, half):
    return lax.dot_general(below, half, (((0,), (0,)), ((), ())), preferred_element_type=F32)


def store_pieces(pieces_ref, slot, total, me):
    count = pieces_ref.shape[0]
    rows = total.shape[0] // count
    for owner in range(count):
        pieces_ref[pl.ds(owner ^ me, 1), slot * rows : (slot + 1) * rows, :] = total[owner * rows : (owner + 1) * rows][None]


def top_kernel(
    gathered_ref, rel_ref, counts_ref, logit_ref, side_ref, cot_ref, colour_ref, head_ref, bias_ref, mats_ref, hidden_ref,
    pieces_ref, half_ref, sums_ref, shaded_ref,
    acc_top, acc_next,
):
    layers = mats_ref.shape[0]
    top = layers - 1
    slots, rays = logit_ref.shape
    parts = rel_ref.shape[0]
    width = head_ref.shape[1]
    block = RAY_BLOCK
    span = slots * block
    head = head_ref[...]
    space = lax.axis_index("space")
    per = rays // parts
    acc_top[...] = jnp.zeros_like(acc_top)
    acc_next[...] = jnp.zeros_like(acc_next)
    sums_ref[...] = jnp.zeros_like(sums_ref)

    for c in range(rays // block):
        at = pl.ds(c * span, span)
        ray_at = pl.ds(c * block, block)
        rank = rel_ref[:, ray_at]
        decays = gathered_ref[:, 0, ray_at]
        products = gathered_ref[:, 1, ray_at]
        ahead = jnp.zeros((parts, block), F32)
        for q in range(parts):
            ahead = ahead + jnp.where(rank[q : q + 1] < rank, decays[q : q + 1], 0.0)
        prefixes = jnp.exp(ahead)
        share = prefixes * products
        tail = jnp.sum(jnp.where(rank > rank[0:1], share, 0.0), axis=0, keepdims=True)
        prefix = prefixes[0:1]

        logit = logit_ref[:, ray_at]
        grown = jnp.exp(-jnp.abs(logit))
        density = jnp.maximum(logit, 0.0) + jnp.log1p(grown)
        slope = jnp.where(logit >= 0, 1.0, grown) / (1.0 + grown)
        place = lax.broadcasted_iota(jnp.int32, (slots, block), 0)
        live = place < counts_ref[:, ray_at]
        optical = jnp.where(live, density * step_length, 0.0)
        reach = jnp.exp(-before_of(optical))
        passed = jnp.exp(-optical)
        blend = reach * (1.0 - passed)
        grad_blend = prefix * side_ref[:, ray_at]
        lost = blend * grad_blend
        after = jnp.zeros_like(lost)
        for j in range(1, slots):
            after = after + jnp.where(place < j, lost[j : j + 1], 0.0)
        grad_optical = reach * passed * grad_blend - after - tail
        grad_logit = jnp.where(live, grad_optical * step_length, 0.0) * slope
        weight = blend * prefix
        weight_sum = jnp.sum(weight, axis=0, keepdims=True)
        cols = columns(
            jnp.concatenate([weight, grad_logit, prefix, weight_sum, jnp.zeros((6, block), F32)], axis=0), block
        )
        cot = cot_ref[ray_at, :]
        shaded = cols[2 * slots] * colour_ref[ray_at, :]
        for n in range(block // per):
            owner = c * (block // per) + n
            shaded_ref[pl.ds((owner ^ space) & 1, 1), pl.ds(owner >> 1, 1)] = shaded[n * per : (n + 1) * per][None, None]
        below = hidden_ref[top, at, :]
        grads = []
        for i in range(slots):
            grads.append((cols[i] * cot + cols[slots + i] * head).astype(BF16))
        logit_sum = jnp.sum(jnp.sum(grad_logit, axis=0, keepdims=True), axis=1, keepdims=True)
        line = jnp.concatenate([grad_logit[i : i + 1] for i in range(slots)], axis=1)
        lines = []
        for _ in range(3):
            lines.append(line.astype(BF16).astype(F32))
            line = line - lines[-1]
        lines = jnp.concatenate(lines + [jnp.zeros((5, span), F32)], axis=0).astype(BF16)
        head_sum = jnp.sum(jnp.dot(lines, below, preferred_element_type=F32), axis=0, keepdims=True)
        bias_sum = jnp.sum(cols[2 * slots + 1] * cot, axis=0, keepdims=True)
        sums_ref[0:1, :] += bias_sum + logit_sum * head
        sums_ref[1:2, :] += head_sum
        sums_ref[3:4, :] += jnp.broadcast_to(logit_sum, (1, width))
        half = jnp.concatenate(grads, axis=0)
        acc_top[...] += mat_grad(below, half)
        half = layer_back(half, below, mats_ref, top)
        sums_ref[2:3, :] += row_sum(half)
        half_ref[at, :] = half
        acc_next[...] += mat_grad(hidden_ref[top - 1, at, :], half)

    me = lax.axis_index("ray")
    store_pieces(pieces_ref, 0, acc_top[...], me)
    store_pieces(pieces_ref, 1, acc_next[...], me)
    mixed = jnp.dot(
        sums_ref[...], mats_ref[top].astype(F32), precision=lax.Precision.HIGHEST, preferred_element_type=F32
    )
    sums_ref[1:2, :] = mixed[1:2, :] + sums_ref[3:4, :] * bias_ref[top : top + 1, :]


def low_kernel(half_ref, sums_ref, mats_ref, hidden_ref, pieces_ref, acc_a, acc_b, bias_ref):
    rows = half_ref.shape[0]
    span = LOW_SPAN
    acc_a[...] = jnp.zeros_like(acc_a)
    acc_b[...] = jnp.zeros_like(acc_b)
    bias_ref[...] = jnp.zeros_like(bias_ref)

    for c in range(rows // span):
        at = pl.ds(c * span, span)
        half = layer_back(half_ref[at, :], hidden_ref[2, at, :], mats_ref, 2)
        bias_ref[0:1, :] += row_sum(half)
        below = hidden_ref[1, at, :]
        acc_a[...] += mat_grad(below, half)
        half = layer_back(half, below, mats_ref, 1)
        bias_ref[1:2, :] += row_sum(half)
        acc_b[...] += mat_grad(hidden_ref[0, at, :], half)

    me = lax.axis_index("ray")
    store_pieces(pieces_ref, 0, acc_a[...], me)
    store_pieces(pieces_ref, 1, acc_b[...], me)
    count = pieces_ref.shape[0]
    first = 2 * (acc_a.shape[0] // count)
    small = jnp.concatenate(
        [sums_ref[0:3, :], bias_ref[0:2, :], jnp.zeros((3, acc_a.shape[1]), F32)], axis=0
    )
    for k in range(count):
        pieces_ref[k, first : first + 8, :] = small


def fold_kernel(step, kept_ref, other_ref, out_ref):
    bit = (lax.axis_index("space") // step) & 1
    for j in range(other_ref.shape[0]):
        out_ref[pl.ds((j & 1) ^ bit, 1), j >> 1] = (kept_ref[0, j] + other_ref[j])[None]


def join_kernel(*refs):
    *inputs, small_ref, kept_ref, other_ref, out_ref, bias_ref, head_ref, composite_ref = refs
    me = lax.axis_index("ray")
    layers, width = out_ref.shape[:2]
    count = len(inputs) // 2
    rows = width // count
    for chunk in range(2):
        for k in range(count):
            piece = inputs[chunk * count + k]
            at = pl.ds(pl.multiple_of((me ^ k) * rows, rows), rows)
            for slot in range(2):
                out_ref[layers - 1 - 2 * chunk - slot, at, :] = piece[slot * rows : (slot + 1) * rows, :]
    first = 2 * rows
    bias_ref[...] = jnp.concatenate(
        [small_ref[first + n : first + n + 1, :] for n in (4, 3, 2, 0)], axis=0
    )
    head_ref[...] = small_ref[first + 1 : first + 2, :]
    composite_ref[...] = kept_ref[0, 0] + other_ref[0]


def partners(count, k):
    return [(i, i ^ k) for i in range(count)]


def on_device(
    grid_table, weights, biases, density_head, sample_cells, sample_counts, ray_order, cotangent
):
    table = grid_table[0]
    mats = weights[0]
    bias = biases[0]
    slots = sample_cells.shape[2]
    cells = sample_cells[0].T.reshape(slots, -1, RAY_BLOCK).transpose(1, 0, 2).reshape(-1, RAY_BLOCK)
    counts = sample_counts.T
    order = ray_order.T
    parts = lax.axis_size("space")
    ray_parts = lax.axis_size("ray")
    layers, width = bias.shape
    rays = sample_cells.shape[1]
    rows = slots * rays
    span = slots * RAY_BLOCK
    shape = jax.ShapeDtypeStruct
    grant = pltpu.CompilerParams(vmem_limit_bytes=GRANT)

    inputs = (cells, counts, order, table, mats, bias, density_head, cotangent)
    hidden, logit, side, pack, rel, colour, counts, mats, bias, head, cot = pl.pallas_call(
        forward_kernel,
        out_shape=(
            shape((layers, rows, width), BF16),
            shape((slots, rays), F32),
            shape((slots, rays), F32),
            shape((2, rays), F32),
            shape((parts, rays), jnp.int32),
            shape((rays, width), F32),
            shape(counts.shape, jnp.int32),
            shape(mats.shape, BF16),
            shape(bias.shape, F32),
            shape(density_head.shape, F32),
            shape(cotangent.shape, F32),
        ),
        in_specs=[HBM] * 8,
        out_specs=(VMEM,) * 11,
        scratch_shapes=[
            pltpu.SMEM(cells.shape, jnp.int32),
            pltpu.VMEM(cells.shape, jnp.int32),
            pltpu.VMEM((parts, rays), jnp.int32),
            pltpu.VMEM(table.shape, BF16),
            pltpu.VMEM((2 * table.shape[0], width // 2), F32),
            pltpu.VMEM((2 * span, width // 2), F32),
            pltpu.SemaphoreType.DMA((6,)),
            pltpu.SemaphoreType.DMA((4,)),
            pltpu.SemaphoreType.DMA((2,)),
        ],
        compiler_params=grant,
        name="forward",
    )(*[pltpu.with_memory_space_constraint(x, pltpu.HBM) for x in inputs])

    gathered = pack[None]
    step = 1
    while step < parts:
        other = lax.ppermute(gathered, "space", partners(parts, step))
        gathered = jnp.concatenate([gathered, other], axis=0)
        step *= 2

    piece_rows = width // ray_parts
    top_pieces, half, sums, shaded = pl.pallas_call(
        top_kernel,
        out_shape=(
            shape((ray_parts, 2 * piece_rows, width), F32),
            shape((rows, width), BF16),
            shape((8, width), F32),
            shape((2, parts // 2, rays // parts, width), F32),
        ),
        in_specs=[VMEM] * 11,
        out_specs=(VMEM,) * 4,
        scratch_shapes=[pltpu.VMEM((width, width), F32)] * 2,
        compiler_params=grant,
        name="top",
    )(gathered, rel, counts, logit, side, cot, colour, head, bias, mats, hidden)

    def shift(array, axis, count, k):
        return lax.ppermute(array, axis, partners(count, k))

    top_got = [shift(top_pieces[k], "ray", ray_parts, k) for k in range(1, ray_parts)]

    low_pieces = pl.pallas_call(
        low_kernel,
        out_shape=shape((ray_parts, 2 * piece_rows + 8, width), F32),
        in_specs=[VMEM] * 4,
        out_specs=VMEM,
        scratch_shapes=[pltpu.VMEM((width, width), F32)] * 2 + [pltpu.VMEM((8, width), F32)],
        compiler_params=grant,
        name="low",
    )(half, sums, mats, hidden)

    low_got = [shift(low_pieces[k], "ray", ray_parts, k) for k in range(1, ray_parts)]

    top_own = top_pieces[0] + sum(top_got[1:], top_got[0])
    low_own = low_pieces[0] + sum(low_got[1:], low_got[0])
    small = low_own
    low_own = low_own[: 2 * piece_rows]
    top_all = [top_own] + [shift(top_own, "ray", ray_parts, k) for k in range(1, ray_parts)]
    low_all = [low_own] + [shift(low_own, "ray", ray_parts, k) for k in range(1, ray_parts)]

    step = 1
    other = shift(shaded[1], "space", parts, step)
    while 2 * step < parts:
        step *= 2
        count, per = other.shape[0], other.shape[1]
        shaded = pl.pallas_call(
            functools.partial(fold_kernel, step),
            out_shape=shape((2, count // 2, per, width), F32),
            in_specs=[VMEM] * 2,
            out_specs=VMEM,
            compiler_params=pltpu.CompilerParams(vmem_limit_bytes=4 << 20),
            name="fold",
        )(shaded, other)
        other = shift(shaded[1], "space", parts, step)

    weight_grads, bias_grads, head_grads, composite = pl.pallas_call(
        join_kernel,
        out_shape=(
            shape((layers, width, width), F32),
            shape((layers, width), F32),
            shape((1, width), F32),
            shape((rays // parts, width), F32),
        ),
        in_specs=[VMEM] * (2 * ray_parts + 3),
        out_specs=(VMEM,) * 4,
        compiler_params=pltpu.CompilerParams(vmem_limit_bytes=8 << 20),
        name="join",
    )(*top_all, *low_all, small, shaded, other)

    return (composite, weight_grads[None], bias_grads[None], head_grads)


def solution(mesh):
    placed = (
        P("space", None, None),
        P("space", None, None, None),
        P("space", None, None),
        P("space", None),
        P("space", "ray", None),
        P("ray", "space"),
        P("ray", None),
        P("ray", None),
    )
    return jax.shard_map(
        on_device,
        mesh=mesh,
        in_specs=placed,
        out_specs=(
            P(("ray", "space"), None),
            P("space", None, None, None),
            P("space", None, None),
            P("space", None),
        ),
        check_vma=False,
    )
```
